256 devices in a mesh: gx: 4 (over x), gy: 4 (over z_hi), gz: 16 (over y, z_lo, core).
Axes of the slice: x: 4, y: 4, z: 8 (z_hi: 4, z_lo: 2; z = z_hi * 2 + z_lo), core: 2. Of those that a mesh axis runs over, the one named last changes fastest.
Arguments:
- position: float32 [3, 4, 4, 256, 128], P(None, 'gx', 'gy', 'gz'), may hold values from 0 to 1
- velocity: float32 [3, 4, 4, 256, 128], P(None, 'gx', 'gy', 'gz'), may hold values from -4 to 4
- radius: float32 [4, 4, 256, 128], P('gx', 'gy', 'gz'), may hold values from 0.06 to 0.1
- cell_count: int32 [4, 4, 256], P('gx', 'gy', 'gz'), may hold values from 16 to 128, as said below
- gas_velocity: float32 [3, 32, 32, 2048], P(None, 'gx', 'gy', 'gz'), may hold values from -3 to 3
- pressure: float32 [32, 32, 2048], P('gx', 'gy', 'gz'), may hold values from -5 to 5
Outputs:
- particle_position: float32 [3, 4, 4, 256, 128], P(None, 'gx', 'gy', 'gz')
- particle_velocity: float32 [3, 4, 4, 256, 128], P(None, 'gx', 'gy', 'gz')
- new_gas_velocity: float32 [3, 32, 32, 2048], P(None, 'gx', 'gy', 'gz')
- new_pressure: float32 [32, 32, 2048], P('gx', 'gy', 'gz')
The draws below stay inside these ranges and needn't reach their ends.
Inputs may be any that keep to these rules, and one draw needn't show every extreme that they name: Slots 0 to cell_count - 1 of a DEM cell hold its particles, the others are empty.
All inputs are finite; a program needn't handle non-finite values.
Results may differ from the reference program's by a relative error of at most 0.0003.
Values sent between devices are 32-bit elements; how exact they have to be, the bound alone decides.
No kernel may reach another device: no remote copies, remote signals or barrier semaphores. Data moves between devices by JAX's collectives and lax.ppermute only.
A program may use at most 64 MiB of HBM per device.

```python
import math
import jax
import jax.numpy as jnp
from jax import lax

S = 128
PZ = 16
B = 8
SUBSTEPS = 2
SWEEPS = 3
NCX = 4
NCY = 4
NL = 256
NX = 32
NY = 32
NZ = 2048
N_GZ = 16


def draw_cell_count(key, part):
    row_index = jnp.arange(NL, dtype=jnp.int32)
    height = row_index % PZ * (NL // PZ) + row_index // PZ
    baseline = S - 3 * S * height // (4 * NL)
    jitter = jax.random.randint(key, (NCX, NCY, NL), -(S // 4), S // 8 + 1, dtype=jnp.int32)
    counts = jnp.clip(baseline[None, None, :] + jitter, S // 8, S)
    counts = counts.at[0, 0, 0].set(S)
    counts = counts.at[0, 0, NL - 1].set(S // 8)
    return counts.astype(jnp.int32)


def block_levels(stream_key, shape, shards, low, high):
    def one(dim, shards_of):
        heights = jax.random.uniform(jax.random.fold_in(jax.random.fold_in(stream_key, 6), dim), (shards_of,), jnp.float32, low / len(shards), high / len(shards))
        return jnp.repeat(jnp.exp(heights), shape[dim] // shards_of).reshape((-1,) + (1,) * (len(shape) - dim - 1))

    factor_of = one(*shards[0])
    for cut in shards[1:]:
        factor_of = factor_of * one(*cut)
    return factor_of


def gaussian(rng, dims, deviation, reach, cuts=(), held_as=jnp.bfloat16):
    values = jax.random.normal(rng, dims, jnp.float32) * deviation
    if len(cuts) > 0:
        values = block_levels(rng, dims, cuts, -0.22, 0.18) * values
    return jnp.clip(values, min=-reach, max=reach).astype(held_as)


def setup_inputs(seed: int = 0) -> dict:
    streams_of = jax.random.split(jax.random.key(seed), 7)
    position = jnp.clip(1.0 * jax.random.uniform(streams_of[0], (3, NCX, NCY, NL, S), jnp.float32) ** block_levels(streams_of[0], (3, NCX, NCY, NL, S), ((1, 4), (2, 4), (3, 16)), -0.2, 0.2), 0.0, 1.0)
    velocity = gaussian(streams_of[1], (3, NCX, NCY, NL, S), 1.0, 4.0, ((1, 4), (2, 4), (3, 16)), jnp.float32)
    radius = jnp.clip(0.06 + 0.040000003 * jax.random.uniform(streams_of[2], (NCX, NCY, NL, S), jnp.float32) ** block_levels(streams_of[2], (NCX, NCY, NL, S), ((0, 4), (1, 4), (2, 16)), -0.2, 0.2), 0.06, 0.1)
    cell_count = draw_cell_count(jax.random.fold_in(streams_of[6], 71), 0)
    gas_velocity = gaussian(streams_of[4], (3, NX, NY, NZ), 0.5, 3.0, ((1, 4), (2, 4), (3, 16)), jnp.float32)
    pressure = gaussian(streams_of[5], (NX, NY, NZ), 1.0, 5.0, ((0, 4), (1, 4), (2, 16)), jnp.float32)
    return dict(position=position, velocity=velocity, radius=radius, cell_count=cell_count, gas_velocity=gas_velocity, pressure=pressure)


SPRING = 1.0
DAMPING = 0.5
TIME_STEP = 0.005
GRAVITY = 1.0
SOFTENING = 0.0025
GAS_STEP = 0.2
GAS_DRAG = 2.0
PARTICLE_DRAG = 4.0
COUPLE_STEP = 0.25
LOWER_BOUND = 0.2
UPPER_BOUND = 2.0
UNIT_STEPS = ((1, 0, 0), (0, 1, 0), (0, 0, 1))

def chebyshev_factor(sweep_index, sweeps):
    centre = 0.5 * (UPPER_BOUND + LOWER_BOUND)
    radius_half = 0.5 * (UPPER_BOUND - LOWER_BOUND)
    return 1.0 / (centre + radius_half * math.cos(math.pi * (2 * sweep_index + 1) / (2 * sweeps)))

def cell_offsets():
    neighbour = jnp.arange(27, dtype=jnp.int32)
    return jnp.stack([neighbour // 9 - 1, neighbour // 3 % 3 - 1, neighbour % 3 - 1]).astype(jnp.float32)

def cell_accel(own_cell, near_cells):
    slots_count = own_cell.shape[-1]
    offsets = cell_offsets()
    centres = near_cells[0:3] + offsets[:, :, None]
    separation = centres[:, :, :, None] - own_cell[0:3][:, None, None, :]
    distance = jnp.sqrt(lax.optimization_barrier(jnp.sum(separation * separation, axis=0)) + SOFTENING)
    normal = separation / distance
    intersection = near_cells[6][:, :, None] + own_cell[6][None, None, :] - distance
    neighbour = jnp.arange(27, dtype=jnp.int32)[:, None, None]
    slot_near = jnp.arange(slots_count, dtype=jnp.int32)[None, :, None]
    slot_own = jnp.arange(slots_count, dtype=jnp.int32)[None, None, :]
    itself = (neighbour == 13) & (slot_near == slot_own)
    active = near_cells[7][:, :, None] * own_cell[7][None, None, :] * jnp.where(itself, 0.0, 1.0)
    pressing = jnp.maximum(intersection, 0.0) * active
    closing = lax.optimization_barrier(jnp.sum((near_cells[3:6][:, :, :, None] - own_cell[3:6][:, None, None, :]) * normal, axis=0))
    magnitude = pressing * (SPRING - DAMPING * closing)
    contact_force = -lax.optimization_barrier(jnp.sum(magnitude[None] * normal, axis=(1, 2)))
    radius_own = own_cell[6]
    return contact_force / (radius_own * radius_own * radius_own)

def move_particles(particle_state, acceleration):
    downward = jnp.array([0.0, 0.0, GRAVITY], dtype=jnp.float32).reshape((3,) + (1,) * (particle_state.ndim - 1))
    new_speed = particle_state[3:6] + TIME_STEP * (acceleration - downward)
    new_place = particle_state[0:3] + TIME_STEP * new_speed
    return jnp.concatenate([new_place, new_speed, particle_state[6:8]], axis=0)

def spread(coordinate, edge_cells):
    centres = jnp.arange(edge_cells, dtype=jnp.float32) + 0.5
    gap_cells = coordinate[..., None] * edge_cells - centres
    kernel = jnp.exp(-gap_cells * gap_cells)
    return kernel / lax.optimization_barrier(jnp.sum(kernel, axis=-1, keepdims=True))

def to_physical(rows_layout):
    leading = rows_layout.shape[:-2]
    slots_count = rows_layout.shape[-1]
    grouped = rows_layout.reshape(leading + (N_GZ, PZ, slots_count))
    return jnp.swapaxes(grouped, -3, -2).reshape(leading + (NL, slots_count))

def to_rows(physical):
    leading = physical.shape[:-2]
    slots_count = physical.shape[-1]
    grouped = physical.reshape(leading + (PZ, N_GZ, slots_count))
    return jnp.swapaxes(grouped, -3, -2).reshape(leading + (NL, slots_count))

def contact_substep(particle_state):
    padded = jnp.pad(particle_state, ((0, 0), (1, 1), (1, 1), (1, 1), (0, 0)))
    cells_x = particle_state.shape[1]
    cells_y = particle_state.shape[2]
    layers = particle_state.shape[3]
    slots_count = particle_state.shape[4]

    def one_cell(cell_index):
        column_x = cell_index // (cells_y * layers)
        column_y = cell_index // layers % cells_y
        layer_index = cell_index % layers
        corner = (jnp.int32(0), column_x, column_y, layer_index, jnp.int32(0))
        own_cell = lax.dynamic_slice(particle_state, corner, (8, 1, 1, 1, slots_count)).reshape(8, slots_count)
        near_cells = lax.dynamic_slice(padded, corner, (8, 3, 3, 3, slots_count)).reshape(8, 27, slots_count)
        return cell_accel(own_cell, near_cells)
    acceleration = lax.map(one_cell, jnp.arange(cells_x * cells_y * layers, dtype=jnp.int32))
    acceleration = jnp.moveaxis(acceleration, 0, 1).reshape(3, cells_x, cells_y, layers, slots_count)
    return move_particles(particle_state, acceleration)

def deposit_column(column, edge_cells):
    weight_x = spread(column[0], edge_cells)
    weight_y = spread(column[1], edge_cells)
    weight_z = spread(column[2], edge_cells)
    volume = 4.0 * math.pi / 3.0 * edge_cells ** 3 * column[6] * column[6] * column[6] * column[7]
    sources = jnp.stack([volume, volume * column[3], volume * column[4], volume * column[5]])
    blocks = jnp.einsum('fls,lsx,lsy,lsz->fxylz', sources, weight_x, weight_y, weight_z, precision=lax.Precision.HIGHEST)
    return blocks.reshape(4, edge_cells, edge_cells, -1)

def sample_column(column, field_column, edge_cells):
    weight_x = spread(column[0], edge_cells)
    weight_y = spread(column[1], edge_cells)
    weight_z = spread(column[2], edge_cells)
    shaped = field_column.reshape(field_column.shape[0], edge_cells, edge_cells, -1, edge_cells)
    return jnp.einsum('fxylz,lsx,lsy,lsz->fls', shaped, weight_x, weight_y, weight_z, precision=lax.Precision.HIGHEST)

def columns_to_grid(column_data):
    fields_count = column_data.shape[1]
    shaped = column_data.reshape(NCX, NCY, fields_count, B, B, NZ)
    return jnp.transpose(shaped, (2, 0, 3, 1, 4, 5)).reshape(fields_count, NX, NY, NZ)

def grid_to_columns(grid_data):
    fields_count = grid_data.shape[0]
    shaped = grid_data.reshape(fields_count, NCX, B, NCY, B, NZ)
    return jnp.transpose(shaped, (1, 3, 0, 2, 4, 5)).reshape(NCX * NCY, fields_count, B, B, NZ)

def interior(padded, margin, offset_cells):
    sizes_inner = [padded.shape[padded.ndim - 3 + axis_index] - 2 * margin for axis_index in range(3)]
    starts = [margin + offset_cells[axis_index] for axis_index in range(3)]
    return padded[..., starts[0]:starts[0] + sizes_inner[0], starts[1]:starts[1] + sizes_inner[1], starts[2]:starts[2] + sizes_inner[2]]

def centred(padded, margin, direction):
    forward = UNIT_STEPS[direction]
    backward = tuple((-component for component in forward))
    return (interior(padded, margin, forward) - interior(padded, margin, backward)) * 0.5

def neighbours(padded, margin):
    summed = interior(padded, margin, (1, 0, 0)) + interior(padded, margin, (-1, 0, 0))
    summed = summed + interior(padded, margin, (0, 1, 0)) + interior(padded, margin, (0, -1, 0))
    return summed + interior(padded, margin, (0, 0, 1)) + interior(padded, margin, (0, 0, -1))

def pad_cells(field_data):
    return jnp.pad(field_data, [(0, 0)] * (field_data.ndim - 3) + [(1, 1)] * 3)

def gas_reference(deposits, gas_velocity, pressure):
    solids = deposits[0]
    momentum = deposits[1:4]
    voidage = 1.0 / (1.0 + solids)
    padded = pad_cells(gas_velocity)
    transport = sum((gas_velocity[direction] * centred(padded, 1, direction) for direction in range(3)))
    intermediate = (voidage * gas_velocity - GAS_STEP * voidage * transport + GAS_STEP * GAS_DRAG * momentum) / (voidage + GAS_STEP * GAS_DRAG * solids)
    flux_padded = pad_cells(voidage * intermediate)
    divergence = sum((centred(flux_padded[direction], 1, direction) for direction in range(3)))
    source = -divergence / GAS_STEP
    diagonal = 6.0 + voidage
    current = pressure
    for sweep_index in range(SWEEPS):
        factor = chebyshev_factor(sweep_index, SWEEPS)
        current = current + factor * (source - diagonal * current + neighbours(pad_cells(current), 1)) / diagonal
    final_padded = pad_cells(current)
    gradient = jnp.stack([centred(final_padded, 1, direction) for direction in range(3)])
    return (intermediate - GAS_STEP * gradient, current, gradient)

def reference(position, velocity, radius, cell_count, gas_velocity, pressure):
    slots_count = position.shape[-1]
    live_slots = (jnp.arange(slots_count, dtype=jnp.int32) < cell_count[..., None]).astype(jnp.float32)
    particle_state = jnp.concatenate([position, velocity, radius[None], live_slots[None]], axis=0)
    particle_state = to_physical(particle_state)
    for substep in range(SUBSTEPS):
        particle_state = contact_substep(particle_state)
    columns = jnp.moveaxis(particle_state.reshape(8, NCX * NCY, NL, slots_count), 1, 0)
    deposit_columns = lax.map(lambda column: deposit_column(column, B), columns)
    deposits = columns_to_grid(deposit_columns)
    new_velocity, new_pressure, gradient = gas_reference(deposits, gas_velocity, pressure)
    field_columns = grid_to_columns(jnp.concatenate([new_velocity, gradient], axis=0))
    sampled = lax.map(lambda column_pair: sample_column(column_pair[0], column_pair[1], B), (columns, field_columns))
    sampled = jnp.moveaxis(sampled, 0, 1).reshape(6, NCX, NCY, NL, slots_count)
    final_speed = (particle_state[3:6] + COUPLE_STEP * (PARTICLE_DRAG * sampled[0:3] - sampled[3:6])) / (1.0 + COUPLE_STEP * PARTICLE_DRAG)
    return (to_rows(particle_state[0:3]), to_rows(final_speed), new_velocity, new_pressure)
```

```python
import math

import jax
import jax.numpy as jnp
from jax import lax
from jax.experimental import pallas as pl
from jax.experimental.pallas import tpu as pltpu
from jax.sharding import PartitionSpec as P

B = 8
S = 128
PZ = 16
SWEEPS = 3
DAMPING = 0.5
TIME_STEP = 0.005
GRAVITY = 1.0
SOFTENING = 0.0025
GAS_STEP = 0.2
GAS_DRAG = 2.0
PARTICLE_DRAG = 4.0
COUPLE_STEP = 0.25
LOWER_BOUND = 0.2
UPPER_BOUND = 2.0
UNIT_STEPS = ((1, 0, 0), (0, 1, 0), (0, 0, 1))

REACH = 0.194
FAR = 1e30
LZ = PZ + 2
NEAR = tuple((dx, dy, dz) for dx in (-1, 0, 1) for dy in (-1, 0, 1) for dz in (-1, 0, 1))
HIGHEST = lax.Precision.HIGHEST


def shift_pair(array_low, array_high, axis):
    count = lax.axis_size(axis)
    forward = [(i, i + 1) for i in range(count - 1)]
    backward = [(i + 1, i) for i in range(count - 1)]
    from_below = lax.ppermute(array_high, axis, forward)
    from_above = lax.ppermute(array_low, axis, backward)
    return from_below, from_above


def with_halo(block, sides, width):
    for axis, dim in sides:
        size = block.shape[dim]
        low, high = shift_pair(
            lax.slice_in_dim(block, 0, width, axis=dim),
            lax.slice_in_dim(block, size - width, size, axis=dim),
            axis,
        )
        block = jnp.concatenate([low, block, high], axis=dim)
    return block


def chebyshev_factor(sweep_index, sweeps):
    centre = 0.5 * (UPPER_BOUND + LOWER_BOUND)
    radius_half = 0.5 * (UPPER_BOUND - LOWER_BOUND)
    return 1.0 / (centre + radius_half * math.cos(math.pi * (2 * sweep_index + 1) / (2 * sweeps)))


def lane_iota(rows):
    return lax.broadcasted_iota(jnp.int32, (rows, S), 1)


def axis_weights(row):
    centres = lax.broadcasted_iota(jnp.int32, (B, S), 0).astype(jnp.float32) + 0.5
    gap = jnp.broadcast_to(row, (B, S)) * float(B) - centres
    kernel = jnp.exp(-gap * gap)
    return kernel / jnp.sum(kernel, axis=0, keepdims=True)


def plane_weights(row_x, row_y):
    wx = axis_weights(row_x)
    wy = axis_weights(row_y)
    return jnp.concatenate(
        [jnp.broadcast_to(wx[a : a + 1], (B, S)) * wy for a in range(B)], axis=0
    )


def contact_kernel(deposit, *refs):
    p_own, p_ylo, p_yhi, p_xlo, p_xhi, r_own, r_ylo, r_yhi, r_xlo, r_xhi = refs[:10]
    out_ref = refs[10]
    rest = refs[11:]
    if deposit:
        dep_ref = rest[0]
        rest = rest[1:]
    mask_s, pref_s, work_s, key_s, list_s, own_s, force_s, rows_s, slots_s = rest[:9]

    def source(dx, dy):
        if dx == 0:
            return ((p_ylo, p_own, p_yhi)[dy + 1], 0, (r_ylo, r_own, r_yhi)[dy + 1], 6 * LZ)
        p_ref, r_ref = (p_xlo, r_xlo) if dx < 0 else (p_xhi, r_xhi)
        return (
            p_ref,
            (dy + 1) * (p_ref.shape[0] // 3),
            r_ref,
            (dy + 1) * (r_ref.shape[0] // 3) + 6 * LZ,
        )

    lane = lane_iota(8)
    tri_row = lax.broadcasted_iota(jnp.int32, (S, 2 * S), 0)
    tri_col = lax.broadcasted_iota(jnp.int32, (S, 2 * S), 1)
    tri = jnp.where((tri_row < tri_col) | (tri_col >= S), 1.0, 0.0).astype(jnp.bfloat16)

    for half in range(2):
        first = 1 + 8 * half
        own_r = r_own[6 * LZ + first : 6 * LZ + first + 8, :]
        own_live = own_r > 0.0
        bounds = []
        for f in range(3):
            value = p_own[f * LZ + first : f * LZ + first + 8, :]
            top = jnp.max(jnp.where(own_live, value, -FAR), axis=1, keepdims=True) + REACH
            bottom = jnp.min(jnp.where(own_live, value, FAR), axis=1, keepdims=True) - REACH
            bounds.append((jnp.broadcast_to(bottom, (8, S)), jnp.broadcast_to(top, (8, S))))
        used = jnp.max(
            jnp.where(own_live, (lane + 1).astype(jnp.float32), 0.0), axis=1, keepdims=True
        )
        for k, offset in enumerate(NEAR):
            p_ref, p_base, r_ref, r_base = source(offset[0], offset[1])
            row = first + offset[2]
            keep = r_ref[r_base + row : r_base + row + 8, :] > 0.0
            for f in range(3):
                start = p_base + f * LZ + row
                value = p_ref[start : start + 8, :] + float(offset[f])
                keep = keep & (value >= bounds[f][0]) & (value <= bounds[f][1])
            mask_s[k * 8 : k * 8 + 8, :] = jnp.where(keep, 1.0, 0.0)
        pref_s[...] = jnp.dot(
            mask_s[...].astype(jnp.bfloat16), tri, preferred_element_type=jnp.float32
        )
        base = jnp.zeros((8, S), jnp.int32)
        for k, offset in enumerate(NEAR):
            before = pref_s[k * 8 : k * 8 + 8, 0:S].astype(jnp.int32)
            count = pref_s[k * 8 : k * 8 + 8, S : 2 * S].astype(jnp.int32)
            hop = jnp.where(mask_s[k * 8 : k * 8 + 8, :] > 0.0, lane - before, 0)
            for bit in range(7):
                step = 1 << bit
                moved = pltpu.roll(hop, S - step, 1)
                hop = jnp.where(
                    (moved & step) != 0, moved, jnp.where((hop & step) != 0, 0, hop)
                )
            slot = (lane - base) & (S - 1)
            pick = (jnp.take_along_axis(hop, slot, axis=1) + slot) & (S - 1)
            page = (base >> 7) + jnp.where(lane < (base & (S - 1)), 1, 0)
            key_s[k * 8 : k * 8 + 8, :] = jnp.where(slot < count, page, -1)
            base = base + count
            p_ref, p_base, r_ref, r_base = source(offset[0], offset[1])
            row = first + offset[2]
            for f in range(7):
                if f < 6:
                    start = p_base + f * LZ + row
                    value = p_ref[start : start + 8, :]
                    if f < 3 and offset[f] != 0:
                        value = value + float(offset[f])
                else:
                    value = r_ref[r_base + row : r_base + row + 8, :]
                work_s[k, f] = jnp.take_along_axis(value, pick, axis=1)
        total = base.astype(jnp.float32)
        pages = (jnp.max(total).astype(jnp.int32) + (S - 1)) >> 7
        for i in range(8):
            rows_s[half * 8 + i] = (
                jnp.max(total[i : i + 1, :]).astype(jnp.int32) + (S - 1)
            ) >> 7
            slots_s[half * 8 + i] = jnp.max(used[i : i + 1, :]).astype(jnp.int32)

        def merge(page, carry):
            acc = [jnp.zeros((8, S), jnp.float32)] * 6 + [jnp.full((8, S), -10.0, jnp.float32)]
            for k in range(27):
                here = key_s[k * 8 : k * 8 + 8, :] == page
                acc = [jnp.where(here, work_s[k, f], acc[f]) for f in range(7)]
            for f in range(7):
                list_s[page, f, half * 8 : half * 8 + 8, :] = acc[f]
            return carry

        lax.fori_loop(0, pages, merge, 0)

    live = r_own[6 * LZ + 1 : 6 * LZ + 17, :] > 0.0
    radius = r_own[6 * LZ + 1 : 6 * LZ + 17, :]
    own_rows = [p_own[f * LZ + 1 : f * LZ + 17, :] for f in range(6)]
    own_rows.append(jnp.where(live, radius, -10.0))
    own_rows.append(jnp.zeros((16, S), jnp.float32))
    own_s[...] = jnp.concatenate(own_rows, axis=0).T
    force_s[...] = jnp.zeros((S, S), jnp.float32)

    def one_cell(cell, carry):
        page_count = rows_s[cell]
        slot_count = slots_s[cell]
        for group in range(4):

            @pl.when(slot_count > 32 * group)
            def _():
                own = []
                for t in range(4):
                    tile = own_s[32 * group + 8 * t : 32 * group + 8 * t + 8, :]
                    own.append(
                        [
                            jnp.take_along_axis(
                                tile, jnp.full((8, S), f * 16, jnp.int32) + cell, axis=1
                            )
                            for f in range(7)
                        ]
                    )

                def near_page(page, acc):
                    near = [
                        jnp.broadcast_to(list_s[page, f, pl.ds(cell, 1), :], (8, S))
                        for f in range(7)
                    ]
                    out = []
                    for t in range(4):
                        ex = near[0] - own[t][0]
                        ey = near[1] - own[t][1]
                        ez = near[2] - own[t][2]
                        square = ex * ex + ey * ey + ez * ez + SOFTENING
                        inverse = lax.rsqrt(square)
                        press = jnp.maximum((near[6] + own[t][6]) - square * inverse, 0.0)
                        closing = (
                            (near[3] - own[t][3]) * ex
                            + (near[4] - own[t][4]) * ey
                            + (near[5] - own[t][5]) * ez
                        )
                        size = press * inverse * (1.0 - DAMPING * (closing * inverse))
                        out.append(acc[3 * t] + size * ex)
                        out.append(acc[3 * t + 1] + size * ey)
                        out.append(acc[3 * t + 2] + size * ez)
                    return tuple(out)

                zero = jnp.zeros((8, S), jnp.float32)
                acc = lax.fori_loop(0, page_count, near_page, (zero,) * 12)
                for t in range(4):
                    rows = slice(32 * group + 8 * t, 32 * group + 8 * t + 8)
                    tile = force_s[rows, :]
                    for f in range(3):
                        total_f = jnp.sum(acc[3 * t + f], axis=1, keepdims=True)
                        tile = jnp.where(
                            lane == f * 16 + cell, jnp.broadcast_to(total_f, (8, S)), tile
                        )
                    force_s[rows, :] = tile

        return carry

    lax.fori_loop(0, PZ, one_cell, 0)

    force = force_s[...].T
    scale = jnp.where(live, -1.0 / (radius * radius * radius), 0.0)
    for f in range(3):
        push = force[f * 16 : f * 16 + 16, :] * scale
        if f == 2:
            push = push - GRAVITY
        speed = p_own[(3 + f) * LZ + 1 : (3 + f) * LZ + 17, :] + TIME_STEP * push
        place = p_own[f * LZ + 1 : f * LZ + 17, :] + TIME_STEP * speed
        out_ref[f * 16 : f * 16 + 16, :] = place
        out_ref[(3 + f) * 16 : (3 + f) * 16 + 16, :] = speed

    if deposit:
        dep_s = rest[9]

        def one_deposit(cell, carry):
            def row(f):
                return out_ref[pl.ds(f * 16 + cell, 1), :]

            r = r_own[pl.ds(6 * LZ + 1 + cell, 1), :]
            volume = (4.0 * math.pi / 3.0 * B**3) * (r * r * r)
            plane = plane_weights(row(0), row(1))
            wz = axis_weights(row(2))
            carried = [volume, volume * row(3), volume * row(4), volume * row(5)]
            left = jnp.concatenate(
                [jnp.broadcast_to(c, (B, S)) * wz for c in carried], axis=0
            )
            block = lax.dot_general(
                left,
                plane,
                (((1,), (1,)), ((), ())),
                precision=HIGHEST,
                preferred_element_type=jnp.float32,
            )
            for f in range(4):
                dep_s[f, pl.ds(pl.multiple_of(cell * 8, 8), 8), 0:64] = block[
                    f * 8 : f * 8 + 8, :
                ]
            return carry

        lax.fori_loop(0, PZ, one_deposit, 0)
        for f in range(4):
            dep_ref[f * 64 : f * 64 + 64, :] = dep_s[f].T[0:64, :]


def contact(deposit, places, radii):
    shapes = [jax.ShapeDtypeStruct((96, S), jnp.float32)]
    scratch = [
        pltpu.VMEM((27 * 8, S), jnp.float32),
        pltpu.VMEM((27 * 8, 2 * S), jnp.float32),
        pltpu.VMEM((27, 7, 8, S), jnp.float32),
        pltpu.VMEM((27 * 8, S), jnp.int32),
        pltpu.VMEM((27, 7, 16, S), jnp.float32),
        pltpu.VMEM((S, S), jnp.float32),
        pltpu.VMEM((S, S), jnp.float32),
        pltpu.SMEM((16,), jnp.int32),
        pltpu.SMEM((16,), jnp.int32),
    ]
    if deposit:
        shapes.append(jax.ShapeDtypeStruct((256, S), jnp.float32))
        scratch.append(pltpu.VMEM((4, S, S), jnp.float32))
    return pl.pallas_call(
        lambda *refs: contact_kernel(deposit, *refs),
        out_shape=shapes,
        scratch_shapes=scratch,
        name="contact_deposit" if deposit else "contact",
    )(*places, *radii)


def sample_kernel(field_ref, state_ref, out_ref, field_s, pair_s, sum_s):
    for v in range(3):
        field_s[:, v * S : v * S + S] = field_ref[v * S : v * S + S, :].T
    pair_s[...] = jnp.zeros((S, 2 * S), jnp.float32)

    def one_cell(cell, carry):
        def row(f):
            return state_ref[pl.ds(f * 16 + cell, 1), :]

        plane = plane_weights(row(0), row(1))
        wz = axis_weights(row(2))
        pair_s[0:64, 0:S] = plane
        pair_s[64:S, S : 2 * S] = plane
        start = pl.multiple_of(cell * 8, 8)
        left = jnp.concatenate(
            [field_s[pl.ds(start, 8), v * S : v * S + S] for v in range(3)], axis=0
        )
        part = jnp.dot(
            left, pair_s[...], precision=HIGHEST, preferred_element_type=jnp.float32
        )
        for v in range(3):
            for odd in range(2):
                value = part[v * 8 : v * 8 + 8, odd * S : odd * S + S] * wz
                sum_s[pl.ds((2 * v + odd) * 16 + cell, 1), :] = jnp.sum(
                    value, axis=0, keepdims=True
                )
        return carry

    lax.fori_loop(0, PZ, one_cell, 0)
    for f in range(3):
        speed = state_ref[(3 + f) * 16 : (3 + f) * 16 + 16, :]
        gas = sum_s[f * 16 : f * 16 + 16, :]
        slope = sum_s[(3 + f) * 16 : (3 + f) * 16 + 16, :]
        out_ref[f * 16 : f * 16 + 16, :] = (
            speed + COUPLE_STEP * (PARTICLE_DRAG * gas - slope)
        ) / (1.0 + COUPLE_STEP * PARTICLE_DRAG)


def sample(fields, state):
    return pl.pallas_call(
        sample_kernel,
        out_shape=jax.ShapeDtypeStruct((48, S), jnp.float32),
        scratch_shapes=[
            pltpu.VMEM((S, 3 * S), jnp.float32),
            pltpu.VMEM((S, 2 * S), jnp.float32),
            pltpu.VMEM((96, S), jnp.float32),
        ],
        name="sample",
    )(fields, state)


def inner(padded, offset=(0, 0, 0)):
    sizes = padded.shape[-3:]
    return padded[
        ...,
        1 + offset[0] : sizes[0] - 1 + offset[0],
        1 + offset[1] : sizes[1] - 1 + offset[1],
        1 + offset[2] : sizes[2] - 1 + offset[2],
    ]


def centred(padded, direction):
    forward = UNIT_STEPS[direction]
    backward = tuple(-c for c in forward)
    return (inner(padded, forward) - inner(padded, backward)) * 0.5


def neighbours(padded):
    return sum(
        inner(padded, tuple(sign * c for c in step)) for step in UNIT_STEPS for sign in (1, -1)
    )


def inside(width):
    keep = None
    for dim, (axis, size) in enumerate((("gx", B), ("gy", B), ("gz", S))):
        index = lax.broadcasted_iota(
            jnp.int32, (B + 2 * width, B + 2 * width, S + 2 * width), dim
        )
        place = lax.axis_index(axis) * size + index - width
        good = (place >= 0) & (place < lax.axis_size(axis) * size)
        keep = good if keep is None else keep & good
    return keep


def gas_inputs(gas_velocity, pressure):
    wide = with_halo(
        jnp.concatenate([gas_velocity, pressure[None]], axis=0),
        (("gy", 2), ("gx", 1), ("gz", 3)),
        5,
    )
    velocity = wide[:3]
    middle = inner(velocity)
    transport = sum(middle[d] * centred(velocity, d) for d in range(3))
    return middle - GAS_STEP * transport, inner(wide[3])


def gas_step(deposits, pulled, pressure):
    wide = with_halo(deposits, (("gy", 2), ("gx", 1), ("gz", 3)), 4)
    solids = wide[0]
    voidage = 1.0 / (1.0 + solids)
    intermediate = (voidage * pulled + GAS_STEP * GAS_DRAG * wide[1:4]) / (
        voidage + GAS_STEP * GAS_DRAG * solids
    )
    flux = voidage * intermediate
    source = -sum(centred(flux[d], d) for d in range(3)) / GAS_STEP
    diagonal = inner(6.0 + voidage)
    current = pressure
    for sweep in range(SWEEPS):
        if sweep > 0:
            source = inner(source)
            diagonal = inner(diagonal)
        factor = chebyshev_factor(sweep, SWEEPS)
        middle = inner(current)
        updated = middle + factor * (
            source - diagonal * middle + neighbours(current)
        ) / diagonal
        current = jnp.where(inside(3 - sweep), updated, 0.0)
    gradient = jnp.stack([centred(current, d) for d in range(3)])
    return intermediate[:, 4:-4, 4:-4, 4:-4] - GAS_STEP * gradient, inner(current), gradient


def body(position, velocity, radius, cell_count, gas_velocity, pressure):
    rank = lax.axis_index("gz")
    ranks = lax.axis_size("gz")
    live = jnp.arange(S, dtype=jnp.int32) < cell_count[0, 0][:, None]
    kept = jnp.where(live, radius[0, 0], 0.0)
    state = jnp.concatenate([position[:, 0, 0], velocity[:, 0, 0], kept[None]], axis=0)
    rows = jnp.swapaxes(state, 0, 1)
    blank = jnp.zeros_like(rows[:1])
    below = jnp.concatenate([blank, rows[:-1]], axis=0)
    above = jnp.concatenate([rows[1:], blank], axis=0)
    extra = jnp.where(rank == ranks - 1, below, jnp.where(rank == 0, above, 0.0))
    sent = jnp.stack([rows, extra], axis=1).reshape(PZ, 14 * S)
    got = lax.all_to_all(sent, "gz", split_axis=0, concat_axis=0, tiled=True)
    got = got.reshape(PZ, 2, 7, S)
    layers = jnp.concatenate([got[PZ - 1 :, 1], got[:, 0], got[:1, 1]], axis=0)
    own = jnp.swapaxes(layers, 0, 1).reshape(7 * LZ, S)

    pulled, wide_pressure = gas_inputs(gas_velocity, pressure)

    def around(block):
        ylo, yhi = shift_pair(block, block, "gy")
        column = jnp.concatenate([ylo, block, yhi], axis=0)
        xlo, xhi = shift_pair(column, column, "gx")
        return (block, ylo, yhi, xlo, xhi)

    first = around(own)
    (moved,) = contact(False, first, first)
    moved = moved.reshape(6, PZ, S)
    zlo, zhi = shift_pair(moved[:, :1], moved[:, PZ - 1 :], "gz")
    middle = jnp.concatenate([zlo, moved, zhi], axis=1).reshape(6 * LZ, S)
    second = around(middle)
    final, deposits = contact(True, second, first)

    new_velocity, new_pressure, gradient = gas_step(
        deposits.reshape(4, B, B, S), pulled, wide_pressure
    )
    fields = jnp.concatenate([new_velocity, gradient], axis=0).reshape(6 * B * B, S)
    speed = sample(fields, final)

    def back(array):
        count = array.shape[0] // PZ
        sent_back = jnp.swapaxes(array.reshape(count, PZ, S), 0, 1).reshape(PZ, count * S)
        returned = lax.all_to_all(sent_back, "gz", split_axis=0, concat_axis=0, tiled=True)
        return jnp.swapaxes(returned.reshape(PZ, count, S), 0, 1)[:, None, None]

    return (back(final[:48]), back(speed), new_velocity, new_pressure)


def solution(mesh):
    placed = (
        P(None, "gx", "gy", "gz", None),
        P(None, "gx", "gy", "gz", None),
        P("gx", "gy", "gz", None),
        P("gx", "gy", "gz"),
        P(None, "gx", "gy", "gz"),
        P("gx", "gy", "gz"),
    )
    return jax.shard_map(
        body,
        mesh=mesh,
        in_specs=placed,
        out_specs=(
            P(None, "gx", "gy", "gz", None),
            P(None, "gx", "gy", "gz", None),
            P(None, "gx", "gy", "gz"),
            P("gx", "gy", "gz"),
        ),
        check_vma=False,
    )
```

```python
import math

import jax
import jax.numpy as jnp
from jax import lax
from jax.experimental import pallas as pl
from jax.experimental.pallas import tpu as pltpu
from jax.sharding import PartitionSpec as P

B = 8
S = 128
PZ = 16
SWEEPS = 3
DAMPING = 0.5
TIME_STEP = 0.005
GRAVITY = 1.0
SOFTENING = 0.0025
GAS_STEP = 0.2
GAS_DRAG = 2.0
PARTICLE_DRAG = 4.0
COUPLE_STEP = 0.25
LOWER_BOUND = 0.2
UPPER_BOUND = 2.0

REACH = 0.194
FAR = 1e30
NEAR = tuple((dx, dy, dz) for dx in (-1, 0, 1) for dy in (-1, 0, 1) for dz in (-1, 0, 1))
HIGHEST = lax.Precision.HIGHEST

L0 = PZ + 6
L1 = PZ + 4
L2 = PZ + 2
RADIUS_ROW = 6 * L0
WG = 5
WD = 4


def shift_pair(array_low, array_high, axis):
    count = lax.axis_size(axis)
    forward = [(i, i + 1) for i in range(count - 1)]
    backward = [(i + 1, i) for i in range(count - 1)]
    from_below = lax.ppermute(array_high, axis, forward)
    from_above = lax.ppermute(array_low, axis, backward)
    return from_below, from_above


def chebyshev_factor(sweep_index, sweeps):
    centre = 0.5 * (UPPER_BOUND + LOWER_BOUND)
    radius_half = 0.5 * (UPPER_BOUND - LOWER_BOUND)
    return 1.0 / (centre + radius_half * math.cos(math.pi * (2 * sweep_index + 1) / (2 * sweeps)))


def lane_iota(rows):
    return lax.broadcasted_iota(jnp.int32, (rows, S), 1)


def axis_weights(row):
    centres = lax.broadcasted_iota(jnp.int32, (B, S), 0).astype(jnp.float32) + 0.5
    gap = jnp.broadcast_to(row, (B, S)) * float(B) - centres
    kernel = jnp.exp(-gap * gap)
    return kernel / jnp.sum(kernel, axis=0, keepdims=True)


def plane_weights(row_x, row_y):
    wx = axis_weights(row_x)
    wy = axis_weights(row_y)
    return jnp.concatenate(
        [jnp.broadcast_to(wx[a : a + 1], (B, S)) * wy for a in range(B)], axis=0
    )


def contact_kernel(cells, deposit, *refs):
    p_own, p_ylo, p_yhi, p_xlo, p_xhi, r_own, r_ylo, r_yhi, r_xlo, r_xhi = refs[:10]
    out_ref = refs[10]
    rest = refs[11:]
    if deposit:
        dep_ref, dep_lo_ref, dep_hi_ref = rest[:3]
        rest = rest[3:]
    mask_s, pref_s, work_s, key_s, list_s, own_s, cell_s, acc_s, force_s, rows_s, slots_s = rest[:11]
    layers = cells + 2
    shift = (L0 - cells) // 2
    block = 7 * L0 if cells == L1 else 6 * L1

    def source(dx, dy):
        if dx == 0:
            return ((p_ylo, p_own, p_yhi)[dy + 1], 0, (r_ylo, r_own, r_yhi)[dy + 1], RADIUS_ROW)
        p_ref, r_ref = (p_xlo, r_xlo) if dx < 0 else (p_xhi, r_xhi)
        return p_ref, (dy + 1) * block, r_ref, (dy + 1) * 7 * L0 + RADIUS_ROW

    lane = lane_iota(8)
    tri_row = lax.broadcasted_iota(jnp.int32, (S, 2 * S), 0)
    tri_col = lax.broadcasted_iota(jnp.int32, (S, 2 * S), 1)
    tri = jnp.where((tri_row < tri_col) | (tri_col >= S), 1.0, 0.0).astype(jnp.bfloat16)

    for start in (0, 8, cells - 8):
        own_r = r_own[RADIUS_ROW + shift + start : RADIUS_ROW + shift + start + 8, :]
        own_live = own_r > 0.0
        bounds = []
        for f in range(3):
            first = f * layers + 1 + start
            value = p_own[first : first + 8, :]
            top = jnp.max(jnp.where(own_live, value, -FAR), axis=1, keepdims=True) + REACH
            bottom = jnp.min(jnp.where(own_live, value, FAR), axis=1, keepdims=True) - REACH
            bounds.append((jnp.broadcast_to(bottom, (8, S)), jnp.broadcast_to(top, (8, S))))
        used = jnp.max(
            jnp.where(own_live, (lane + 1).astype(jnp.float32), 0.0), axis=1, keepdims=True
        )
        for k, offset in enumerate(NEAR):
            p_ref, p_base, r_ref, r_base = source(offset[0], offset[1])
            row = r_base + shift + start + offset[2]
            keep = r_ref[row : row + 8, :] > 0.0
            for f in range(3):
                row = p_base + f * layers + 1 + start + offset[2]
                value = p_ref[row : row + 8, :] + float(offset[f])
                keep = keep & (value >= bounds[f][0]) & (value <= bounds[f][1])
            mask_s[k * 8 : k * 8 + 8, :] = jnp.where(keep, 1.0, 0.0)
        pref_s[...] = jnp.dot(
            mask_s[...].astype(jnp.bfloat16), tri, preferred_element_type=jnp.float32
        )
        base = jnp.zeros((8, S), jnp.int32)
        for k, offset in enumerate(NEAR):
            before = pref_s[k * 8 : k * 8 + 8, 0:S].astype(jnp.int32)
            count = pref_s[k * 8 : k * 8 + 8, S : 2 * S].astype(jnp.int32)
            hop = jnp.where(mask_s[k * 8 : k * 8 + 8, :] > 0.0, lane - before, 0)
            for bit in range(7):
                step = 1 << bit
                moved = pltpu.roll(hop, S - step, 1)
                hop = jnp.where(
                    (moved & step) != 0, moved, jnp.where((hop & step) != 0, 0, hop)
                )
            slot = (lane - base) & (S - 1)
            pick = (jnp.take_along_axis(hop, slot, axis=1) + slot) & (S - 1)
            page = (base >> 7) + jnp.where(lane < (base & (S - 1)), 1, 0)
            key_s[k * 8 : k * 8 + 8, :] = jnp.where(slot < count, page, -1)
            base = base + count
            p_ref, p_base, r_ref, r_base = source(offset[0], offset[1])
            for f in range(7):
                if f < 6:
                    row = p_base + f * layers + 1 + start + offset[2]
                    value = p_ref[row : row + 8, :]
                    if f < 3 and offset[f] != 0:
                        value = value + float(offset[f])
                else:
                    row = r_base + shift + start + offset[2]
                    value = r_ref[row : row + 8, :]
                work_s[k, f] = jnp.take_along_axis(value, pick, axis=1)
        total = base.astype(jnp.float32)
        pages = (jnp.max(total).astype(jnp.int32) + (S - 1)) >> 7
        for i in range(8):
            rows_s[start + i] = (
                jnp.max(total[i : i + 1, :]).astype(jnp.int32) + (S - 1)
            ) >> 7
            slots_s[start + i] = jnp.max(used[i : i + 1, :]).astype(jnp.int32)

        def merge(page, carry):
            acc = [jnp.zeros((8, S), jnp.float32)] * 6 + [jnp.full((8, S), -10.0, jnp.float32)]
            for k in range(27):
                here = key_s[k * 8 : k * 8 + 8, :] == page
                acc = [jnp.where(here, work_s[k, f], acc[f]) for f in range(7)]
            for f in range(7):
                list_s[page, f, start : start + 8, :] = acc[f]
            return carry

        lax.fori_loop(0, pages, merge, 0)

    radius = r_own[RADIUS_ROW + shift : RADIUS_ROW + shift + cells, :]
    live = radius > 0.0
    own_s[...] = jnp.zeros((2 * S, S), jnp.float32)
    for f in range(6):
        own_s[f * 32 : f * 32 + cells, :] = p_own[f * layers + 1 : f * layers + 1 + cells, :]
    own_s[6 * 32 : 6 * 32 + cells, :] = jnp.where(live, radius, -10.0)
    turned = (own_s[0:S, :].T, own_s[S : 2 * S, :].T)
    own_s[0:S, :] = turned[0]
    own_s[S : 2 * S, :] = turned[1]
    force_s[...] = jnp.zeros((S, S), jnp.float32)

    def cell_forces(cell, page_count, tiles):
        for t in range(tiles):
            for f in range(7):
                tile = own_s[(f // 4) * S + 8 * t : (f // 4) * S + 8 * t + 8, :]
                cell_s[t, f] = jnp.take_along_axis(
                    tile, jnp.full((8, S), (f % 4) * 32, jnp.int32) + cell, axis=1
                )

        def near_page(page, fresh):
            near = [
                jnp.broadcast_to(list_s[page, f, pl.ds(cell, 1), :], (8, S)) for f in range(7)
            ]
            for t in range(tiles):
                ex = near[0] - cell_s[t, 0]
                ey = near[1] - cell_s[t, 1]
                ez = near[2] - cell_s[t, 2]
                square = ex * ex + ey * ey + ez * ez + SOFTENING
                inverse = lax.rsqrt(square)
                press = jnp.maximum((near[6] + cell_s[t, 6]) - square * inverse, 0.0)
                closing = (
                    (near[3] - cell_s[t, 3]) * ex
                    + (near[4] - cell_s[t, 4]) * ey
                    + (near[5] - cell_s[t, 5]) * ez
                )
                size = press * inverse * (1.0 - DAMPING * (closing * inverse))
                for f, part in enumerate((size * ex, size * ey, size * ez)):
                    acc_s[t, f] = part if fresh else acc_s[t, f] + part

        near_page(0, True)

        def more(page, carry):
            near_page(page, False)
            return carry

        lax.fori_loop(1, page_count, more, 0)
        for t in range(tiles):
            rows = slice(8 * t, 8 * t + 8)
            tile = force_s[rows, :]
            for f in range(3):
                total_f = jnp.sum(acc_s[t, f], axis=1, keepdims=True)
                tile = jnp.where(
                    lane == f * 32 + cell, jnp.broadcast_to(total_f, (8, S)), tile
                )
            force_s[rows, :] = tile

    def one_cell(cell, carry):
        page_count = rows_s[cell]
        slot_count = slots_s[cell]
        for tiles in (4, 8, 12, 16):

            @pl.when((slot_count > 8 * tiles - 32) & (slot_count <= 8 * tiles))
            def _():
                cell_forces(cell, page_count, tiles)

        return carry

    lax.fori_loop(0, cells, one_cell, 0)

    force = force_s[...].T
    scale = jnp.where(live, -1.0 / (radius * radius * radius), 0.0)
    for f in range(3):
        push = force[f * 32 : f * 32 + cells, :] * scale
        if f == 2:
            push = push - GRAVITY
        first = (3 + f) * layers + 1
        speed = p_own[first : first + cells, :] + TIME_STEP * push
        first = f * layers + 1
        place = p_own[first : first + cells, :] + TIME_STEP * speed
        out_ref[f * cells : f * cells + cells, :] = place
        out_ref[(3 + f) * cells : (3 + f) * cells + cells, :] = speed

    if deposit:
        dep_s, edge_s = rest[11:13]

        def one_deposit(cell):
            def row(f):
                return out_ref[pl.ds(f * cells + cell, 1), :]

            r = r_own[pl.ds(RADIUS_ROW + shift + cell, 1), :]
            volume = (4.0 * math.pi / 3.0 * B**3) * (r * r * r)
            plane = plane_weights(row(0), row(1))
            wz = axis_weights(row(2))
            carried = [volume, volume * row(3), volume * row(4), volume * row(5)]
            left = jnp.concatenate(
                [jnp.broadcast_to(c, (B, S)) * wz for c in carried], axis=0
            )
            return lax.dot_general(
                left,
                plane,
                (((1,), (1,)), ((), ())),
                precision=HIGHEST,
                preferred_element_type=jnp.float32,
            )

        def some_deposits(step, carry):
            blocks = [one_deposit(step * 3 + i) for i in range(3)]
            for i in range(3):
                for f in range(4):
                    dep_s[f, pl.ds(pl.multiple_of(step * 24 + i * 8, 8), 8), 0:64] = blocks[i][
                        f * 8 : f * 8 + 8, :
                    ]
            return carry

        lax.fori_loop(0, cells // 3, some_deposits, 0)
        edge_s[...] = jnp.zeros((S, S), jnp.float32)
        for f in range(4):
            edge_s[f * 32 : f * 32 + 8, :] = dep_s[f, B + S : B + S + 8, :]
            edge_s[f * 32 + 24 : f * 32 + 32, :] = dep_s[f, 0:B, :]
        for f in range(5):
            grid = (dep_s[f, B : B + S, :] if f < 4 else edge_s[...]).T
            dep_ref[f * 64 : f * 64 + 64, :] = grid[0:64, :]
            for x in range(B):
                row = (f * B + x) * WD
                dep_lo_ref[row : row + WD, :] = grid[x * B : x * B + WD, :]
                dep_hi_ref[row : row + WD, :] = grid[x * B + B - WD : x * B + B, :]


def contact(cells, deposit, places, radii):
    shapes = [jax.ShapeDtypeStruct((6 * cells, S), jnp.float32)]
    scratch = [
        pltpu.VMEM((27 * 8, S), jnp.float32),
        pltpu.VMEM((27 * 8, 2 * S), jnp.float32),
        pltpu.VMEM((27, 7, 8, S), jnp.float32),
        pltpu.VMEM((27 * 8, S), jnp.int32),
        pltpu.VMEM((27, 7, 24, S), jnp.float32),
        pltpu.VMEM((2 * S, S), jnp.float32),
        pltpu.VMEM((16, 7, 8, S), jnp.float32),
        pltpu.VMEM((16, 3, 8, S), jnp.float32),
        pltpu.VMEM((S, S), jnp.float32),
        pltpu.SMEM((24,), jnp.int32),
        pltpu.SMEM((24,), jnp.int32),
    ]
    if deposit:
        shapes.append(jax.ShapeDtypeStruct((5 * 64, S), jnp.float32))
        shapes += [jax.ShapeDtypeStruct((5 * B * WD, S), jnp.float32)] * 2
        scratch += [pltpu.VMEM((4, S + 2 * B, S), jnp.float32), pltpu.VMEM((S, S), jnp.float32)]
    return pl.pallas_call(
        lambda *refs: contact_kernel(cells, deposit, *refs),
        out_shape=shapes,
        scratch_shapes=scratch,
        name="contact_deposit" if deposit else "contact",
    )(*places, *radii)


def assemble(target, edge, own, ylo, yhi, xlo, xhi, y_at, x_at, width):
    span = B + 2 * width

    def put(field, x, y, value):
        rows = slice(y, y + value.shape[0])
        if field < 4:
            target[field, x, rows, 0:S] = value
        else:
            edge[x, rows, :] = value

    for field in range(5):
        for x in range(B):
            row = (field * B + x) * B
            put(field, width + x, width, own[row : row + B, :])
            row = y_at + (field * B + x) * width
            put(field, width + x, 0, ylo[row : row + width, :])
            put(field, width + x, width + B, yhi[row : row + width, :])
        for x in range(width):
            for place, ref in ((x, xlo), (width + B + x, xhi)):
                row = x_at + (field * width + x) * B
                put(field, place, width, ref[row : row + B, :])
                row = x_at + 5 * width * B + (field * width + x) * width
                put(field, place, 0, ref[row : row + width, :])
                row += 5 * width * width
                put(field, place, width + B, ref[row : row + width, :])
    lane = lane_iota(8)
    for field in range(4):
        index = field * 32 + jnp.where(
            lane < 64, jnp.minimum(lane, 15), jnp.maximum(lane - 96, 16)
        )
        for x in range(span):
            for y in range(0, edge.shape[1], 8):
                target[field, x, y : y + 8, S : 2 * S] = jnp.take_along_axis(
                    edge[x, y : y + 8, :], index, axis=1
                )


def gas_kernel(*refs):
    (
        rank_ref,
        g_own,
        g_ylo,
        g_yhi,
        g_xlo,
        g_xhi,
        d_own,
        d_ylo,
        d_yhi,
        d_xlo,
        d_xhi,
        state_ref,
        sent_ref,
        newv_ref,
        newp_ref,
        u_s,
        ue_s,
        d_s,
        de_s,
        flux_s,
        mid_s,
        inv_s,
        src_s,
        pa_s,
        pb_s,
        grad_s,
        field_s,
        pair_s,
        sum_s,
    ) = refs
    assemble(u_s, ue_s, g_own, g_ylo, g_yhi, g_xlo, g_xhi, 6 * L1, 18 * L1, WG)
    assemble(d_s, de_s, d_own, d_ylo, d_yhi, d_xlo, d_xhi, 0, 0, WD)
    wide = B + 2 * WD
    ring = 2 * S

    def zdiff(value):
        return pltpu.roll(value, ring - 1, 1) - pltpu.roll(value, 1, 1)

    def zsum(value):
        return pltpu.roll(value, ring - 1, 1) + pltpu.roll(value, 1, 1)

    def ydiff(value):
        return pltpu.roll(value, wide - 1, 0) - pltpu.roll(value, 1, 0)

    def ysum(value):
        return pltpu.roll(value, wide - 1, 0) + pltpu.roll(value, 1, 0)

    for x in range(wide):
        speed = [u_s[d, x + 1, 1 : wide + 1, :] for d in range(3)]
        solids = d_s[0, x]
        voidage = 1.0 / (1.0 + solids)
        under = 1.0 / (voidage + GAS_STEP * GAS_DRAG * solids)
        inv_s[x] = 1.0 / (6.0 + voidage)
        for k in range(3):
            slope = speed[0] * (u_s[k, x + 2, 1 : wide + 1, :] - u_s[k, x, 1 : wide + 1, :])
            slope += speed[1] * (u_s[k, x + 1, 2 : wide + 2, :] - u_s[k, x + 1, 0:wide, :])
            slope += speed[2] * zdiff(speed[k])
            pulled = speed[k] - (0.5 * GAS_STEP) * slope
            middle = (voidage * pulled + GAS_STEP * GAS_DRAG * d_s[1 + k, x]) * under
            mid_s[k, x] = middle
            flux_s[k, x] = voidage * middle
        pa_s[x] = u_s[3, x + 1, 1 : wide + 1, :]
    for x in range(1, wide - 1):
        spread = (flux_s[0, x + 1] - flux_s[0, x - 1]) + ydiff(flux_s[1, x]) + zdiff(flux_s[2, x])
        src_s[x] = (-0.5 / GAS_STEP) * spread * inv_s[x]

    row = lax.broadcasted_iota(jnp.int32, (wide, ring), 0) - WD + rank_ref[1] * B
    col = lax.broadcasted_iota(jnp.int32, (wide, ring), 1)
    col = jnp.where(col < ring - 64, col, col - ring) + rank_ref[2] * S
    inside = (row >= 0) & (row < rank_ref[4]) & (col >= 0) & (col < rank_ref[5])
    for sweep in range(SWEEPS):
        old, new = (pa_s, pb_s) if sweep % 2 == 0 else (pb_s, pa_s)
        factor = chebyshev_factor(sweep, SWEEPS)
        for x in range(1 + sweep, wide - 1 - sweep):
            place = rank_ref[0] * B + (x - WD)
            kept = jnp.where((place >= 0) & (place < rank_ref[3]), 1.0, 0.0)
            middle = old[x]
            around = (old[x + 1] + old[x - 1]) + ysum(middle) + zsum(middle)
            value = middle + factor * (src_s[x] + around * inv_s[x] - middle)
            new[x] = jnp.where(inside, value, 0.0) * kept
    last = pb_s if SWEEPS % 2 == 1 else pa_s
    rows = slice(WD, WD + B)
    for x in range(B):
        plane = last[WD + x]
        slopes = (last[WD + x + 1] - last[WD + x - 1], ydiff(plane), zdiff(plane))
        newp_ref[x * B : x * B + B, :] = plane[rows, 0:S]
        for k in range(3):
            slope = 0.5 * slopes[k]
            at = (k * B + x) * B
            grad_s[at : at + B, :] = slope[rows, 0:S]
            newv_ref[at : at + B, :] = (mid_s[k, WD + x] - GAS_STEP * slope)[rows, 0:S]

    joined = (
        newv_ref[0:S, :],
        jnp.concatenate([newv_ref[S : S + 64, :], grad_s[0:64, :]], axis=0),
        grad_s[64:192, :],
    )
    for v in range(3):
        field_s[:, v * S : v * S + S] = joined[v].T
    pair_s[...] = jnp.zeros((4, S, 2 * S), jnp.float32)

    def some_cells(step, carry):
        for i in range(4):
            cell = step * 4 + i

            def row_of(f):
                return state_ref[pl.ds(f * L2 + 1 + cell, 1), :]

            plane_w = plane_weights(row_of(0), row_of(1))
            wz = axis_weights(row_of(2))
            pair_s[i, 0:64, 0:S] = plane_w
            pair_s[i, 64:S, S : 2 * S] = plane_w
            start = pl.multiple_of(cell * 8, 8)
            left = jnp.concatenate(
                [field_s[pl.ds(start, 8), v * S : v * S + S] for v in range(3)], axis=0
            )
            part = jnp.dot(
                left, pair_s[i], precision=HIGHEST, preferred_element_type=jnp.float32
            )
            for v in range(3):
                for odd in range(2):
                    value = part[v * 8 : v * 8 + 8, odd * S : odd * S + S] * wz
                    sum_s[pl.ds((2 * v + odd) * 16 + cell, 1), :] = jnp.sum(
                        value, axis=0, keepdims=True
                    )
        return carry

    lax.fori_loop(0, PZ // 4, some_cells, 0)
    for f in range(3):
        speed = state_ref[(3 + f) * L2 + 1 : (3 + f) * L2 + 17, :]
        gas = sum_s[f * 16 : f * 16 + 16, :]
        slope = sum_s[(3 + f) * 16 : (3 + f) * 16 + 16, :]
        sent_ref[:, f * S : f * S + S] = state_ref[f * L2 + 1 : f * L2 + 17, :]
        sent_ref[:, (3 + f) * S : (3 + f) * S + S] = (
            speed + COUPLE_STEP * (PARTICLE_DRAG * gas - slope)
        ) / (1.0 + COUPLE_STEP * PARTICLE_DRAG)


def gas_and_sample(ranks, gas, deposits, state):
    wide = B + 2 * WD
    ring = 2 * S
    vmem = pl.BlockSpec(memory_space=pltpu.VMEM)
    return pl.pallas_call(
        gas_kernel,
        out_shape=[
            jax.ShapeDtypeStruct((PZ, 6 * S), jnp.float32),
            jax.ShapeDtypeStruct((3 * 64, S), jnp.float32),
            jax.ShapeDtypeStruct((64, S), jnp.float32),
        ],
        in_specs=[pl.BlockSpec(memory_space=pltpu.SMEM)] + [vmem] * 11,
        scratch_shapes=[
            pltpu.VMEM((4, B + 2 * WG, 24, ring), jnp.float32),
            pltpu.VMEM((B + 2 * WG, 24, S), jnp.float32),
            pltpu.VMEM((4, wide, wide, ring), jnp.float32),
            pltpu.VMEM((wide, wide, S), jnp.float32),
            pltpu.VMEM((3, wide, wide, ring), jnp.float32),
            pltpu.VMEM((3, wide, wide, ring), jnp.float32),
            pltpu.VMEM((wide, wide, ring), jnp.float32),
            pltpu.VMEM((wide, wide, ring), jnp.float32),
            pltpu.VMEM((wide, wide, ring), jnp.float32),
            pltpu.VMEM((wide, wide, ring), jnp.float32),
            pltpu.VMEM((3 * 64, S), jnp.float32),
            pltpu.VMEM((S, 3 * S), jnp.float32),
            pltpu.VMEM((4, S, 2 * S), jnp.float32),
            pltpu.VMEM((96, S), jnp.float32),
        ],
        name="gas_sample",
    )(ranks, *gas, *deposits, state)


def body(position, velocity, radius, cell_count, gas_velocity, pressure):
    axes = ("gx", "gy", "gz")
    rank = lax.axis_index("gz")
    count = lax.axis_size("gz")
    ranks = jnp.stack(
        [lax.axis_index(a) for a in axes]
        + [jnp.int32(lax.axis_size(a) * n) for a, n in zip(axes, (B, B, S))]
    )
    live = jnp.arange(S, dtype=jnp.int32) < cell_count[0, 0][:, None]
    kept = jnp.where(live, radius[0, 0], 0.0)
    state = jnp.concatenate([position[:, 0, 0], velocity[:, 0, 0], kept[None]], axis=0)
    rows = jnp.swapaxes(state, 0, 1).reshape(PZ, 7 * S)
    blank = jnp.zeros_like(rows[:1])
    below = jnp.concatenate([blank, rows[:-1]], axis=0)
    above = jnp.concatenate([rows[1:], blank], axis=0)
    extra = jnp.where(rank >= count - 3, below, jnp.where(rank < 3, above, 0.0))
    gas = jnp.concatenate([gas_velocity, pressure[None]], axis=0)
    edge_size = 4 * B * B * WG
    low_edge = gas[..., :WG].reshape(1, edge_size)
    high_edge = gas[..., S - WG :].reshape(1, edge_size)
    target = jnp.arange(PZ, dtype=jnp.int32)[:, None]
    edges = jnp.where(
        target == rank + 1, high_edge, jnp.where(target == rank - 1, low_edge, 0.0)
    )
    sent = jnp.concatenate([rows, extra, edges], axis=1)
    got = lax.all_to_all(sent, "gz", split_axis=0, concat_axis=0, tiled=True)
    layers = jnp.concatenate(
        [got[PZ - 3 :, 7 * S : 14 * S], got[:, : 7 * S], got[:3, 7 * S : 14 * S]], axis=0
    )
    own = jnp.swapaxes(layers.reshape(L0, 7, S), 0, 1).reshape(7 * L0, S)
    from_low = lax.dynamic_index_in_dim(got, jnp.maximum(rank - 1, 0), 0, keepdims=False)
    from_high = lax.dynamic_index_in_dim(got, jnp.minimum(rank + 1, count - 1), 0, keepdims=False)
    zlo = jnp.where(rank > 0, from_low[14 * S :], 0.0).reshape(4, B * B, WG)
    zhi = jnp.where(rank < count - 1, from_high[14 * S :], 0.0).reshape(4, B * B, WG)
    packed = jnp.concatenate([zhi, jnp.zeros((4, B * B, 32 - 2 * WG), jnp.float32), zlo], axis=2)
    packed = jnp.swapaxes(packed, 0, 1).reshape(B * B, S)
    gas5 = jnp.concatenate([gas.reshape(4 * B * B, S), packed], axis=0)

    def y_slab(first):
        return gas5.reshape(5, B, B, S)[:, :, first : first + WG].reshape(5 * B * WG, S)

    def x_slab(ylo, yhi, first, at, width, block):
        parts = [block.reshape(5, B, B * S)[:, first : first + width].reshape(-1, S)]
        for part in (ylo, yhi):
            part = part[at:].reshape(5, B, width * S)[:, first : first + width]
            parts.append(part.reshape(-1, S))
        return parts

    ylo, yhi = shift_pair(own, own, "gy")
    column = jnp.concatenate([ylo, own, yhi], axis=0)
    xlo, xhi = shift_pair(column, column, "gx")
    first = (own, ylo, yhi, xlo, xhi)
    (moved,) = contact(L1, False, first, first)

    ylo, yhi = shift_pair(
        jnp.concatenate([moved, y_slab(0)], axis=0),
        jnp.concatenate([moved, y_slab(B - WG)], axis=0),
        "gy",
    )
    column = [ylo[: 6 * L1], moved, yhi[: 6 * L1]]
    xlo, xhi = shift_pair(
        jnp.concatenate(column + x_slab(ylo, yhi, 0, 6 * L1, WG, gas5), axis=0),
        jnp.concatenate(column + x_slab(ylo, yhi, B - WG, 6 * L1, WG, gas5), axis=0),
        "gx",
    )
    final, dep, dep_low, dep_high = contact(L2, True, (moved, ylo, yhi, xlo, xhi), first)

    dylo, dyhi = shift_pair(dep_low, dep_high, "gy")
    dxlo, dxhi = shift_pair(
        jnp.concatenate(x_slab(dylo, dyhi, 0, 0, WD, dep), axis=0),
        jnp.concatenate(x_slab(dylo, dyhi, B - WD, 0, WD, dep), axis=0),
        "gx",
    )
    sent_back, new_velocity, new_pressure = gas_and_sample(
        ranks, (gas5, ylo, yhi, xlo, xhi), (dep, dylo, dyhi, dxlo, dxhi), final
    )
    returned = lax.all_to_all(sent_back, "gz", split_axis=0, concat_axis=0, tiled=True)
    returned = jnp.swapaxes(returned.reshape(PZ, 6, S), 0, 1)[:, None, None]
    return (
        returned[:3],
        returned[3:],
        new_velocity.reshape(3, B, B, S),
        new_pressure.reshape(B, B, S),
    )


def solution(mesh):
    placed = (
        P(None, "gx", "gy", "gz", None),
        P(None, "gx", "gy", "gz", None),
        P("gx", "gy", "gz", None),
        P("gx", "gy", "gz"),
        P(None, "gx", "gy", "gz"),
        P("gx", "gy", "gz"),
    )
    return jax.shard_map(
        body,
        mesh=mesh,
        in_specs=placed,
        out_specs=(
            P(None, "gx", "gy", "gz", None),
            P(None, "gx", "gy", "gz", None),
            P(None, "gx", "gy", "gz"),
            P("gx", "gy", "gz"),
        ),
        check_vma=False,
    )
```

```python
import math

import jax
import jax.numpy as jnp
from jax import lax
from jax.experimental import pallas as pl
from jax.experimental.pallas import tpu as pltpu
from jax.sharding import PartitionSpec as P

B = 8
S = 128
PZ = 16
SWEEPS = 3
DAMPING = 0.5
TIME_STEP = 0.005
GRAVITY = 1.0
SOFTENING = 0.0025
GAS_STEP = 0.2
GAS_DRAG = 2.0
PARTICLE_DRAG = 4.0
COUPLE_STEP = 0.25
LOWER_BOUND = 0.2
UPPER_BOUND = 2.0

REACH = 0.194
FAR = 1e30
NEAR = tuple((dx, dy, dz) for dx in (-1, 0, 1) for dy in (-1, 0, 1) for dz in (-1, 0, 1))
HIGHEST = lax.Precision.HIGHEST
FLAGS = {}

L0 = PZ + 6
L1 = PZ + 4
L2 = PZ + 2
RADIUS_ROW = 6 * L0
WG = 5
WD = 4


def shift_pair(array_low, array_high, axis):
    count = lax.axis_size(axis)
    forward = [(i, (i + 1) % count) for i in range(count)]
    backward = [((i + 1) % count, i) for i in range(count)]
    from_below = lax.ppermute(array_high, axis, forward)
    from_above = lax.ppermute(array_low, axis, backward)
    return from_below, from_above


def chebyshev_factor(sweep_index, sweeps):
    centre = 0.5 * (UPPER_BOUND + LOWER_BOUND)
    radius_half = 0.5 * (UPPER_BOUND - LOWER_BOUND)
    return 1.0 / (centre + radius_half * math.cos(math.pi * (2 * sweep_index + 1) / (2 * sweeps)))


def has_sides(rank_ref):
    return tuple(
        (rank_ref[d] > 0, rank_ref[d] >= 0, rank_ref[d] < rank_ref[3 + d] // B - 1)
        for d in range(2)
    )


def lane_iota(rows):
    return lax.broadcasted_iota(jnp.int32, (rows, S), 1)


def axis_weights(row):
    centres = lax.broadcasted_iota(jnp.int32, (B, S), 0).astype(jnp.float32) + 0.5
    gap = jnp.broadcast_to(row, (B, S)) * float(B) - centres
    kernel = jnp.exp(-gap * gap)
    return kernel / jnp.sum(kernel, axis=0, keepdims=True)


def plane_weights(row_x, row_y):
    wx = axis_weights(row_x)
    wy = axis_weights(row_y)
    return jnp.concatenate(
        [jnp.broadcast_to(wx[a : a + 1], (B, S)) * wy for a in range(B)], axis=0
    )


def contact_kernel(cells, deposit, *refs):
    rank_ref, p_own, p_ylo, p_yhi, p_xlo, p_xhi, r_own, r_ylo, r_yhi, r_xlo, r_xhi = refs[:11]
    out_ref = refs[11]
    rest = refs[12:]
    if deposit:
        dep_ref, dep_lo_ref, dep_hi_ref = rest[:3]
        rest = rest[3:]
    mask_s, pref_s, work_s, key_s, list_s, own_s, turn_s, pick_s = rest[:8]
    cell_a, cell_b, acc_a, acc_b, force_s, rows_s, slots_s = rest[8:15]
    sides = has_sides(rank_ref)
    least = {
        (dx, dy): jnp.where(sides[0][dx + 1] & sides[1][dy + 1], 0.0, FAR)
        for dx in (-1, 0, 1)
        for dy in (-1, 0, 1)
    }
    layers = cells + 2
    shift = (L0 - cells) // 2
    block = 7 * L0 if cells == L1 else 6 * L1

    def source(dx, dy):
        if dx == 0:
            return ((p_ylo, p_own, p_yhi)[dy + 1], 0, (r_ylo, r_own, r_yhi)[dy + 1], RADIUS_ROW)
        p_ref, r_ref = (p_xlo, r_xlo) if dx < 0 else (p_xhi, r_xhi)
        return p_ref, (dy + 1) * block, r_ref, (dy + 1) * 7 * L0 + RADIUS_ROW

    lane = lane_iota(8)
    tri_row = lax.broadcasted_iota(jnp.int32, (S, 2 * S), 0)
    tri_col = lax.broadcasted_iota(jnp.int32, (S, 2 * S), 1)
    tri = jnp.where((tri_row < tri_col) | (tri_col >= S), 1.0, 0.0).astype(jnp.bfloat16)

    for start in (0, 8, cells - 8):
        own_r = r_own[RADIUS_ROW + shift + start : RADIUS_ROW + shift + start + 8, :]
        own_live = own_r > 0.0
        bounds = []
        for f in range(3):
            first = f * layers + 1 + start
            value = p_own[first : first + 8, :]
            top = jnp.max(jnp.where(own_live, value, -FAR), axis=1, keepdims=True) + REACH
            bottom = jnp.min(jnp.where(own_live, value, FAR), axis=1, keepdims=True) - REACH
            bounds.append((jnp.broadcast_to(bottom, (8, S)), jnp.broadcast_to(top, (8, S))))
        used = jnp.max(
            jnp.where(own_live, (lane + 1).astype(jnp.float32), 0.0), axis=1, keepdims=True
        )
        for k, offset in enumerate(NEAR):
            p_ref, p_base, r_ref, r_base = source(offset[0], offset[1])
            row = r_base + shift + start + offset[2]
            keep = r_ref[row : row + 8, :] > least[offset[:2]]
            for f in range(3):
                row = p_base + f * layers + 1 + start + offset[2]
                value = p_ref[row : row + 8, :] + float(offset[f])
                keep = keep & (value >= bounds[f][0]) & (value <= bounds[f][1])
            mask_s[k * 8 : k * 8 + 8, :] = jnp.where(keep, 1.0, 0.0)
        pref_s[...] = jnp.dot(
            mask_s[...].astype(jnp.bfloat16), tri, preferred_element_type=jnp.float32
        )
        base = jnp.zeros((8, S), jnp.int32)
        for k, offset in enumerate(NEAR):
            before = pref_s[k * 8 : k * 8 + 8, 0:S].astype(jnp.int32)
            count = pref_s[k * 8 : k * 8 + 8, S : 2 * S].astype(jnp.int32)
            hop = jnp.where(mask_s[k * 8 : k * 8 + 8, :] > 0.0, lane - before, 0)
            for bit in range(7):
                step = 1 << bit
                moved = pltpu.roll(hop, S - step, 1)
                hop = jnp.where(
                    (moved & step) != 0, moved, jnp.where((hop & step) != 0, 0, hop)
                )
            slot = (lane - base) & (S - 1)
            pick = (jnp.take_along_axis(hop, slot, axis=1) + slot) & (S - 1)
            page = (base >> 7) + jnp.where(lane < (base & (S - 1)), 1, 0)
            key_s[k * 8 : k * 8 + 8, :] = jnp.where(slot < count, page, -1)
            base = base + count
            p_ref, p_base, r_ref, r_base = source(offset[0], offset[1])
            for f in range(7):
                if f < 6:
                    row = p_base + f * layers + 1 + start + offset[2]
                    value = p_ref[row : row + 8, :]
                    if f < 3 and offset[f] != 0:
                        value = value + float(offset[f])
                else:
                    row = r_base + shift + start + offset[2]
                    value = r_ref[row : row + 8, :]
                work_s[k, f] = jnp.take_along_axis(value, pick, axis=1)
        total = base.astype(jnp.float32)
        pages = (jnp.max(total).astype(jnp.int32) + (S - 1)) >> 7
        for i in range(8):
            rows_s[start + i] = (
                jnp.max(total[i : i + 1, :]).astype(jnp.int32) + (S - 1)
            ) >> 7
            slots_s[start + i] = jnp.max(used[i : i + 1, :]).astype(jnp.int32)

        def merge(page, carry):
            acc = [jnp.zeros((8, S), jnp.float32)] * 6 + [jnp.full((8, S), -10.0, jnp.float32)]
            for k in range(27):
                here = key_s[k * 8 : k * 8 + 8, :] == page
                acc = [jnp.where(here, work_s[k, f], acc[f]) for f in range(7)]
            for f in range(7):
                list_s[page, f, start : start + 8, :] = acc[f]
            return carry

        lax.fori_loop(0, pages, merge, 0)

    radius = r_own[RADIUS_ROW + shift : RADIUS_ROW + shift + cells, :]
    live = radius > 0.0
    own_s[...] = jnp.zeros(own_s.shape, jnp.float32)
    for f in range(7):
        value = (
            p_own[f * layers + 1 : f * layers + 1 + cells, :]
            if f < 6
            else jnp.where(live, radius, -10.0)
        )
        for part in range(3):
            piece = value.astype(jnp.bfloat16).astype(jnp.float32)
            own_s[pl.ds(part * 8 + f, cells, stride=32), :] = piece
            value = value - piece
    for i in range(cells):
        turn_s[i] = own_s[i * 32 : i * 32 + 32, :].T.astype(jnp.bfloat16)
    pick_row = lax.broadcasted_iota(jnp.int32, (32, 7 * S), 0)
    pick_col = lax.broadcasted_iota(jnp.int32, (32, 7 * S), 1)
    chosen = (pick_row < 24) & ((pick_row & 7) == (pick_col >> 7))
    pick_s[...] = jnp.where(chosen, 1.0, 0.0).astype(jnp.bfloat16)
    force_s[...] = jnp.zeros((S, S), jnp.float32)

    def spread_cell(cell, target):
        target[...] = jnp.dot(
            turn_s[cell], pick_s[...], preferred_element_type=jnp.float32
        )

    def near_page(cell, page, values, sums, tiles, fresh):
        near = [jnp.broadcast_to(list_s[page, f, pl.ds(cell, 1), :], (8, S)) for f in range(7)]
        for t in range(tiles):
            rows = slice(8 * t, 8 * t + 8)
            own = [values[rows, f * S : f * S + S] for f in range(7)]
            ex = near[0] - own[0]
            ey = near[1] - own[1]
            ez = near[2] - own[2]
            square = ex * ex + ey * ey + ez * ez + SOFTENING
            inverse = lax.rsqrt(square)
            press = jnp.maximum((near[6] + own[6]) - square * inverse, 0.0)
            closing = (
                (near[3] - own[3]) * ex + (near[4] - own[4]) * ey + (near[5] - own[5]) * ez
            )
            size = press * inverse * (1.0 - DAMPING * (closing * inverse))
            for f, part in enumerate((size * ex, size * ey, size * ez)):
                cols = slice(f * S, f * S + S)
                sums[rows, cols] = part if fresh else sums[rows, cols] + part

    def reduce_cell(cell, sums):
        for t in range(16):
            rows = slice(8 * t, 8 * t + 8)
            tile = force_s[rows, :]
            for f in range(3):
                total_f = jnp.sum(sums[rows, f * S : f * S + S], axis=1, keepdims=True)
                tile = jnp.where(
                    lane == f * 32 + cell, jnp.broadcast_to(total_f, (8, S)), tile
                )
            force_s[rows, :] = tile

    def one_cell(cell, values, next_values, sums, last_sums):
        spread_cell(jnp.minimum(cell + 1, cells - 1), next_values)
        reduce_cell(cell - 1, last_sums)
        near_page(cell, 0, values, sums, 16, True)
        few = slots_s[cell] <= 64
        page_count = rows_s[cell]

        def more(tiles):
            def step(page, carry):
                near_page(cell, page, values, sums, tiles, False)
                return carry

            lax.fori_loop(1, page_count, step, 0)

        @pl.when(few)
        def _():
            more(8)

        @pl.when(jnp.logical_not(few))
        def _():
            more(16)

    def two_cells(pair, carry):
        one_cell(2 * pair, cell_a, cell_b, acc_a, acc_b)
        one_cell(2 * pair + 1, cell_b, cell_a, acc_b, acc_a)
        return carry

    spread_cell(0, cell_a)
    lax.fori_loop(0, cells // 2, two_cells, 0)
    reduce_cell(cells - 1, acc_b)

    force = force_s[...].T
    scale = jnp.where(live, -1.0 / (radius * radius * radius), 0.0)
    for f in range(3):
        push = force[f * 32 : f * 32 + cells, :] * scale
        if f == 2:
            push = push - GRAVITY
        first = (3 + f) * layers + 1
        speed = p_own[first : first + cells, :] + TIME_STEP * push
        first = f * layers + 1
        place = p_own[first : first + cells, :] + TIME_STEP * speed
        out_ref[f * cells : f * cells + cells, :] = place
        out_ref[(3 + f) * cells : (3 + f) * cells + cells, :] = speed

    if deposit:
        dep_s, edge_s = rest[15:17]

        def one_deposit(cell):
            def row(f):
                return out_ref[pl.ds(f * cells + cell, 1), :]

            r = r_own[pl.ds(RADIUS_ROW + shift + cell, 1), :]
            volume = (4.0 * math.pi / 3.0 * B**3) * (r * r * r)
            plane = plane_weights(row(0), row(1))
            wz = axis_weights(row(2))
            carried = [volume, volume * row(3), volume * row(4), volume * row(5)]
            left = jnp.concatenate(
                [jnp.broadcast_to(c, (B, S)) * wz for c in carried], axis=0
            )
            return lax.dot_general(
                left,
                plane,
                (((1,), (1,)), ((), ())),
                precision=HIGHEST,
                preferred_element_type=jnp.float32,
            )

        def some_deposits(step, carry):
            blocks = [one_deposit(step * 3 + i) for i in range(3)]
            for i in range(3):
                for f in range(4):
                    dep_s[f, pl.ds(pl.multiple_of(step * 24 + i * 8, 8), 8), 0:64] = blocks[i][
                        f * 8 : f * 8 + 8, :
                    ]
            return carry

        lax.fori_loop(0, cells // 3, some_deposits, 0)
        edge_s[...] = jnp.zeros((S, S), jnp.float32)
        for f in range(4):
            edge_s[f * 32 : f * 32 + 8, :] = dep_s[f, B + S : B + S + 8, :]
            edge_s[f * 32 + 24 : f * 32 + 32, :] = dep_s[f, 0:B, :]
        for f in range(5):
            grid = (dep_s[f, B : B + S, :] if f < 4 else edge_s[...]).T
            dep_ref[f * 64 : f * 64 + 64, :] = grid[0:64, :]
            for x in range(B):
                row = (f * B + x) * WD
                dep_lo_ref[row : row + WD, :] = grid[x * B : x * B + WD, :]
                dep_hi_ref[row : row + WD, :] = grid[x * B + B - WD : x * B + B, :]


def near(arrays):
    return [pltpu.with_memory_space_constraint(a, pltpu.VMEM) for a in arrays]


def contact(cells, deposit, ranks, places, radii):
    shapes = [pltpu.VMEM((6 * cells, S), jnp.float32)]
    scratch = [
        pltpu.VMEM((27 * 8, S), jnp.float32),
        pltpu.VMEM((27 * 8, 2 * S), jnp.float32),
        pltpu.VMEM((27, 7, 8, S), jnp.float32),
        pltpu.VMEM((27 * 8, S), jnp.int32),
        pltpu.VMEM((27, 7, 24, S), jnp.float32),
        pltpu.VMEM((5 * S, S), jnp.float32),
        pltpu.VMEM((L1, S, 32), jnp.bfloat16),
        pltpu.VMEM((32, 7 * S), jnp.bfloat16),
        pltpu.VMEM((S, 7 * S), jnp.float32),
        pltpu.VMEM((S, 7 * S), jnp.float32),
        pltpu.VMEM((S, 3 * S), jnp.float32),
        pltpu.VMEM((S, 3 * S), jnp.float32),
        pltpu.VMEM((S, S), jnp.float32),
        pltpu.SMEM((24,), jnp.int32),
        pltpu.SMEM((24,), jnp.int32),
    ]
    if deposit:
        shapes.append(pltpu.VMEM((5 * 64, S), jnp.float32))
        shapes += [pltpu.VMEM((5 * B * WD, S), jnp.float32)] * 2
        scratch += [pltpu.VMEM((4, S + 2 * B, S), jnp.float32), pltpu.VMEM((S, S), jnp.float32)]
    return pl.pallas_call(
        lambda *refs: contact_kernel(cells, deposit, *refs),
        out_shape=shapes,
        in_specs=[pl.BlockSpec(memory_space=pltpu.SMEM)]
        + [pl.BlockSpec(memory_space=pltpu.VMEM)] * 10,
        scratch_shapes=scratch,
        compiler_params=pltpu.CompilerParams(flags=FLAGS),
        name="contact_deposit" if deposit else "contact",
    )(ranks, *near(places), *near(radii))


def assemble(target, edge, own, ylo, yhi, xlo, xhi, y_at, x_at, width, weight):
    span = B + 2 * width

    def put(field, x, y, value):
        rows = slice(y, y + value.shape[0])
        if field < 4:
            target[field, x, rows, 0:S] = value
        else:
            edge[x, rows, :] = value

    for field in range(5):
        for x in range(B):
            row = (field * B + x) * B
            put(field, width + x, width, own[row : row + B, :])
            row = y_at + (field * B + x) * width
            put(field, width + x, 0, ylo[row : row + width, :] * weight[0, -1])
            put(field, width + x, width + B, yhi[row : row + width, :] * weight[0, 1])
        for x in range(width):
            for place, ref, side in ((x, xlo, -1), (width + B + x, xhi, 1)):
                row = x_at + (field * width + x) * B
                put(field, place, width, ref[row : row + B, :] * weight[side, 0])
                row = x_at + 5 * width * B + (field * width + x) * width
                put(field, place, 0, ref[row : row + width, :] * weight[side, -1])
                row += 5 * width * width
                put(field, place, width + B, ref[row : row + width, :] * weight[side, 1])
    lane = lane_iota(8)
    for field in range(4):
        index = field * 32 + jnp.where(
            lane < 64, jnp.minimum(lane, 15), jnp.maximum(lane - 96, 16)
        )
        for x in range(span):
            for y in range(0, edge.shape[1], 8):
                target[field, x, y : y + 8, S : 2 * S] = jnp.take_along_axis(
                    edge[x, y : y + 8, :], index, axis=1
                )


def gas_kernel(*refs):
    (
        rank_ref,
        g_own,
        g_ylo,
        g_yhi,
        g_xlo,
        g_xhi,
        d_own,
        d_ylo,
        d_yhi,
        d_xlo,
        d_xhi,
        state_ref,
        sent_ref,
        newv_ref,
        newp_ref,
        u_s,
        ue_s,
        d_s,
        de_s,
        flux_s,
        mid_s,
        inv_s,
        src_s,
        pa_s,
        pb_s,
        grad_s,
        field_s,
        pair_s,
        sum_s,
    ) = refs
    sides = has_sides(rank_ref)
    weight = {
        (dx, dy): jnp.where(sides[0][dx + 1] & sides[1][dy + 1], 1.0, 0.0)
        for dx in (-1, 0, 1)
        for dy in (-1, 0, 1)
    }
    assemble(u_s, ue_s, g_own, g_ylo, g_yhi, g_xlo, g_xhi, 6 * L1, 18 * L1, WG, weight)
    assemble(d_s, de_s, d_own, d_ylo, d_yhi, d_xlo, d_xhi, 0, 0, WD, weight)
    wide = B + 2 * WD
    ring = 2 * S

    def zdiff(value):
        return pltpu.roll(value, ring - 1, 1) - pltpu.roll(value, 1, 1)

    def zsum(value):
        return pltpu.roll(value, ring - 1, 1) + pltpu.roll(value, 1, 1)

    def ydiff(value):
        return pltpu.roll(value, wide - 1, 0) - pltpu.roll(value, 1, 0)

    def ysum(value):
        return pltpu.roll(value, wide - 1, 0) + pltpu.roll(value, 1, 0)

    for x in range(wide):
        speed = [u_s[d, x + 1, 1 : wide + 1, :] for d in range(3)]
        solids = d_s[0, x]
        voidage = 1.0 / (1.0 + solids)
        under = 1.0 / (voidage + GAS_STEP * GAS_DRAG * solids)
        inv_s[x] = 1.0 / (6.0 + voidage)
        for k in range(3):
            slope = speed[0] * (u_s[k, x + 2, 1 : wide + 1, :] - u_s[k, x, 1 : wide + 1, :])
            slope += speed[1] * (u_s[k, x + 1, 2 : wide + 2, :] - u_s[k, x + 1, 0:wide, :])
            slope += speed[2] * zdiff(speed[k])
            pulled = speed[k] - (0.5 * GAS_STEP) * slope
            middle = (voidage * pulled + GAS_STEP * GAS_DRAG * d_s[1 + k, x]) * under
            mid_s[k, x] = middle
            flux_s[k, x] = voidage * middle
        pa_s[x] = u_s[3, x + 1, 1 : wide + 1, :]
    for x in range(1, wide - 1):
        spread = (flux_s[0, x + 1] - flux_s[0, x - 1]) + ydiff(flux_s[1, x]) + zdiff(flux_s[2, x])
        src_s[x] = (-0.5 / GAS_STEP) * spread * inv_s[x]

    row = lax.broadcasted_iota(jnp.int32, (wide, ring), 0) - WD + rank_ref[1] * B
    col = lax.broadcasted_iota(jnp.int32, (wide, ring), 1)
    col = jnp.where(col < ring - 64, col, col - ring) + rank_ref[2] * S
    inside = (row >= 0) & (row < rank_ref[4]) & (col >= 0) & (col < rank_ref[5])
    for sweep in range(SWEEPS):
        old, new = (pa_s, pb_s) if sweep % 2 == 0 else (pb_s, pa_s)
        factor = chebyshev_factor(sweep, SWEEPS)
        for x in range(1 + sweep, wide - 1 - sweep):
            place = rank_ref[0] * B + (x - WD)
            kept = jnp.where((place >= 0) & (place < rank_ref[3]), 1.0, 0.0)
            middle = old[x]
            around = (old[x + 1] + old[x - 1]) + ysum(middle) + zsum(middle)
            value = middle + factor * (src_s[x] + around * inv_s[x] - middle)
            new[x] = jnp.where(inside, value, 0.0) * kept
    last = pb_s if SWEEPS % 2 == 1 else pa_s
    rows = slice(WD, WD + B)
    for x in range(B):
        plane = last[WD + x]
        slopes = (last[WD + x + 1] - last[WD + x - 1], ydiff(plane), zdiff(plane))
        newp_ref[x * B : x * B + B, :] = plane[rows, 0:S]
        for k in range(3):
            slope = 0.5 * slopes[k]
            at = (k * B + x) * B
            grad_s[at : at + B, :] = slope[rows, 0:S]
            newv_ref[at : at + B, :] = (mid_s[k, WD + x] - GAS_STEP * slope)[rows, 0:S]

    joined = (
        newv_ref[0:S, :],
        jnp.concatenate([newv_ref[S : S + 64, :], grad_s[0:64, :]], axis=0),
        grad_s[64:192, :],
    )
    for v in range(3):
        field_s[:, v * S : v * S + S] = joined[v].T
    pair_s[...] = jnp.zeros((4, S, 2 * S), jnp.float32)

    def some_cells(step, carry):
        for i in range(4):
            cell = step * 4 + i

            def row_of(f):
                return state_ref[pl.ds(f * L2 + 1 + cell, 1), :]

            plane_w = plane_weights(row_of(0), row_of(1))
            wz = axis_weights(row_of(2))
            pair_s[i, 0:64, 0:S] = plane_w
            pair_s[i, 64:S, S : 2 * S] = plane_w
            start = pl.multiple_of(cell * 8, 8)
            left = jnp.concatenate(
                [field_s[pl.ds(start, 8), v * S : v * S + S] for v in range(3)], axis=0
            )
            part = jnp.dot(
                left, pair_s[i], precision=HIGHEST, preferred_element_type=jnp.float32
            )
            for v in range(3):
                for odd in range(2):
                    value = part[v * 8 : v * 8 + 8, odd * S : odd * S + S] * wz
                    sum_s[pl.ds((2 * v + odd) * 16 + cell, 1), :] = jnp.sum(
                        value, axis=0, keepdims=True
                    )
        return carry

    lax.fori_loop(0, PZ // 4, some_cells, 0)
    for f in range(3):
        speed = state_ref[(3 + f) * L2 + 1 : (3 + f) * L2 + 17, :]
        gas = sum_s[f * 16 : f * 16 + 16, :]
        slope = sum_s[(3 + f) * 16 : (3 + f) * 16 + 16, :]
        sent_ref[pl.ds(f, PZ, stride=8), :] = state_ref[f * L2 + 1 : f * L2 + 17, :]
        sent_ref[pl.ds(3 + f, PZ, stride=8), :] = (
            speed + COUPLE_STEP * (PARTICLE_DRAG * gas - slope)
        ) / (1.0 + COUPLE_STEP * PARTICLE_DRAG)


def gas_and_sample(ranks, gas, deposits, state):
    wide = B + 2 * WD
    ring = 2 * S
    vmem = pl.BlockSpec(memory_space=pltpu.VMEM)
    return pl.pallas_call(
        gas_kernel,
        out_shape=[
            pltpu.VMEM((PZ * 8, S), jnp.float32),
            jax.ShapeDtypeStruct((3 * 64, S), jnp.float32),
            jax.ShapeDtypeStruct((64, S), jnp.float32),
        ],
        in_specs=[pl.BlockSpec(memory_space=pltpu.SMEM)] + [vmem] * 11,
        scratch_shapes=[
            pltpu.VMEM((4, B + 2 * WG, 24, ring), jnp.float32),
            pltpu.VMEM((B + 2 * WG, 24, S), jnp.float32),
            pltpu.VMEM((4, wide, wide, ring), jnp.float32),
            pltpu.VMEM((wide, wide, S), jnp.float32),
            pltpu.VMEM((3, wide, wide, ring), jnp.float32),
            pltpu.VMEM((3, wide, wide, ring), jnp.float32),
            pltpu.VMEM((wide, wide, ring), jnp.float32),
            pltpu.VMEM((wide, wide, ring), jnp.float32),
            pltpu.VMEM((wide, wide, ring), jnp.float32),
            pltpu.VMEM((wide, wide, ring), jnp.float32),
            pltpu.VMEM((3 * 64, S), jnp.float32),
            pltpu.VMEM((S, 3 * S), jnp.float32),
            pltpu.VMEM((4, S, 2 * S), jnp.float32),
            pltpu.VMEM((96, S), jnp.float32),
        ],
        name="gas_sample",
    )(ranks, *near((*gas, *deposits, state)))


def body(position, velocity, radius, cell_count, gas_velocity, pressure):
    axes = ("gx", "gy", "gz")
    rank = lax.axis_index("gz")
    count = lax.axis_size("gz")
    ranks = jnp.stack(
        [lax.axis_index(a) for a in axes]
        + [jnp.int32(lax.axis_size(a) * n) for a, n in zip(axes, (B, B, S))]
    )
    live = jnp.arange(S, dtype=jnp.int32) < cell_count[0, 0][:, None]
    kept = jnp.where(live, radius[0, 0], 0.0)
    state = jnp.concatenate([position[:, 0, 0], velocity[:, 0, 0], kept[None]], axis=0)
    rows = jnp.swapaxes(state, 0, 1)
    blank = jnp.zeros_like(rows[:1])
    below = jnp.concatenate([blank, rows[:-1]], axis=0)
    above = jnp.concatenate([rows[1:], blank], axis=0)
    extra = jnp.where(rank >= count - 3, below, jnp.where(rank < 3, above, 0.0))
    gas = jnp.concatenate([gas_velocity, pressure[None]], axis=0)
    edge_size = 4 * B * B * WG
    low_edge = gas[..., :WG].reshape(1, edge_size // S, S)
    high_edge = gas[..., S - WG :].reshape(1, edge_size // S, S)
    target = jnp.arange(PZ, dtype=jnp.int32)[:, None, None]
    edges = jnp.where(
        target == rank + 1, high_edge, jnp.where(target == rank - 1, low_edge, 0.0)
    )
    sent = jnp.concatenate([rows, extra, edges], axis=1).reshape(PZ * 24, S)
    got = lax.all_to_all(sent, "gz", split_axis=0, concat_axis=0, tiled=True)
    got = got.reshape(PZ, 24, S)
    layers = jnp.concatenate([got[PZ - 3 :, 7:14], got[:, :7], got[:3, 7:14]], axis=0)
    own = jnp.swapaxes(layers, 0, 1).reshape(7 * L0, S)
    from_low = lax.dynamic_index_in_dim(got, jnp.maximum(rank - 1, 0), 0, keepdims=False)
    from_high = lax.dynamic_index_in_dim(got, jnp.minimum(rank + 1, count - 1), 0, keepdims=False)
    zlo = jnp.where(rank > 0, from_low[14:], 0.0).reshape(4, B * B, WG)
    zhi = jnp.where(rank < count - 1, from_high[14:], 0.0).reshape(4, B * B, WG)
    packed = jnp.concatenate([zhi, jnp.zeros((4, B * B, 32 - 2 * WG), jnp.float32), zlo], axis=2)
    packed = jnp.swapaxes(packed, 0, 1).reshape(B * B, S)
    gas5 = jnp.concatenate([gas.reshape(4 * B * B, S), packed], axis=0)

    def y_slab(first):
        return gas5.reshape(5, B, B, S)[:, :, first : first + WG].reshape(5 * B * WG, S)

    def x_slab(ylo, yhi, first, at, width, block):
        parts = [block.reshape(5, B, B * S)[:, first : first + width].reshape(-1, S)]
        for part in (ylo, yhi):
            part = part[at:].reshape(5, B, width * S)[:, first : first + width]
            parts.append(part.reshape(-1, S))
        return parts

    ylo, yhi = shift_pair(own, own, "gy")
    column = jnp.concatenate([ylo, own, yhi], axis=0)
    xlo, xhi = shift_pair(column, column, "gx")
    first = (own, ylo, yhi, xlo, xhi)
    (moved,) = contact(L1, False, ranks, first, first)

    ylo, yhi = shift_pair(
        jnp.concatenate([moved, y_slab(0)], axis=0),
        jnp.concatenate([moved, y_slab(B - WG)], axis=0),
        "gy",
    )
    column = [ylo[: 6 * L1], moved, yhi[: 6 * L1]]
    xlo, xhi = shift_pair(
        jnp.concatenate(column + x_slab(ylo, yhi, 0, 6 * L1, WG, gas5), axis=0),
        jnp.concatenate(column + x_slab(ylo, yhi, B - WG, 6 * L1, WG, gas5), axis=0),
        "gx",
    )
    final, dep, dep_low, dep_high = contact(L2, True, ranks, (moved, ylo, yhi, xlo, xhi), first)

    dylo, dyhi = shift_pair(dep_low, dep_high, "gy")
    dxlo, dxhi = shift_pair(
        jnp.concatenate(x_slab(dylo, dyhi, 0, 0, WD, dep), axis=0),
        jnp.concatenate(x_slab(dylo, dyhi, B - WD, 0, WD, dep), axis=0),
        "gx",
    )
    sent_back, new_velocity, new_pressure = gas_and_sample(
        ranks, (gas5, ylo, yhi, xlo, xhi), (dep, dylo, dyhi, dxlo, dxhi), final
    )
    returned = lax.all_to_all(sent_back, "gz", split_axis=0, concat_axis=0, tiled=True)
    returned = jnp.swapaxes(returned.reshape(PZ, 8, S)[:, :6], 0, 1)[:, None, None]
    return (
        returned[:3],
        returned[3:],
        new_velocity.reshape(3, B, B, S),
        new_pressure.reshape(B, B, S),
    )


def solution(mesh):
    placed = (
        P(None, "gx", "gy", "gz", None),
        P(None, "gx", "gy", "gz", None),
        P("gx", "gy", "gz", None),
        P("gx", "gy", "gz"),
        P(None, "gx", "gy", "gz"),
        P("gx", "gy", "gz"),
    )
    return jax.shard_map(
        body,
        mesh=mesh,
        in_specs=placed,
        out_specs=(
            P(None, "gx", "gy", "gz", None),
            P(None, "gx", "gy", "gz", None),
            P(None, "gx", "gy", "gz"),
            P("gx", "gy", "gz"),
        ),
        check_vma=False,
    )
```

```python
import math

import jax
import jax.numpy as jnp
from jax import lax
from jax.experimental import pallas as pl
from jax.experimental.pallas import tpu as pltpu
from jax.sharding import PartitionSpec as P

B = 8
S = 128
PZ = 16
SWEEPS = 3
DAMPING = 0.5
TIME_STEP = 0.005
GRAVITY = 1.0
SOFTENING = 0.0025
GAS_STEP = 0.2
GAS_DRAG = 2.0
PARTICLE_DRAG = 4.0
COUPLE_STEP = 0.25
LOWER_BOUND = 0.2
UPPER_BOUND = 2.0

REACH = 0.194
FAR = 1e30
NEAR = tuple((dx, dy, dz) for dx in (-1, 0, 1) for dy in (-1, 0, 1) for dz in (-1, 0, 1))
HIGHEST = lax.Precision.HIGHEST
FLAGS = {}

L0 = PZ + 6
L1 = PZ + 4
L2 = PZ + 2
RADIUS_ROW = 6 * L0
WG = 5
WD = 4


def shift_pair(array_low, array_high, axis):
    count = lax.axis_size(axis)
    forward = [(i, (i + 1) % count) for i in range(count)]
    backward = [((i + 1) % count, i) for i in range(count)]
    from_below = lax.ppermute(array_high, axis, forward)
    from_above = lax.ppermute(array_low, axis, backward)
    return from_below, from_above


def chebyshev_factor(sweep_index, sweeps):
    centre = 0.5 * (UPPER_BOUND + LOWER_BOUND)
    radius_half = 0.5 * (UPPER_BOUND - LOWER_BOUND)
    return 1.0 / (centre + radius_half * math.cos(math.pi * (2 * sweep_index + 1) / (2 * sweeps)))


def has_sides():
    ranks = [lax.axis_index(axis) for axis in ("gx", "gy")]
    sizes = [lax.axis_size(axis) for axis in ("gx", "gy")]
    return tuple((r > 0, r >= 0, r < n - 1) for r, n in zip(ranks, sizes))


def lane_iota(rows):
    return lax.broadcasted_iota(jnp.int32, (rows, S), 1)


def axis_weights(row):
    centres = lax.broadcasted_iota(jnp.int32, (B, S), 0).astype(jnp.float32) + 0.5
    gap = jnp.broadcast_to(row, (B, S)) * float(B) - centres
    kernel = jnp.exp(-gap * gap)
    return kernel / jnp.sum(kernel, axis=0, keepdims=True)


def plane_weights(row_x, row_y):
    wx = axis_weights(row_x)
    wy = axis_weights(row_y)
    return jnp.concatenate(
        [jnp.broadcast_to(wx[a : a + 1], (B, S)) * wy for a in range(B)], axis=0
    )


def contact_kernel(cells, deposit, *refs):
    p_own, p_ylo, p_yhi, p_xlo, p_xhi, r_own, r_ylo, r_yhi, r_xlo, r_xhi = refs[:10]
    out_ref = refs[10]
    rest = refs[11:]
    if deposit:
        dep_ref, dep_lo_ref, dep_hi_ref = rest[:3]
        rest = rest[3:]
    mask_s, pref_s, work_s, key_s, list_s, own_s, turn_s, pick_s = rest[:8]
    cell_a, cell_b, acc_a, acc_b, force_s, rows_s, slots_s = rest[8:15]
    sides = has_sides()
    least = {
        (dx, dy): jnp.where(sides[0][dx + 1] & sides[1][dy + 1], 0.0, FAR)
        for dx in (-1, 0, 1)
        for dy in (-1, 0, 1)
    }
    layers = cells + 2
    shift = (L0 - cells) // 2
    block = 7 * L0 if cells == L1 else 6 * L1

    def source(dx, dy):
        if dx == 0:
            return ((p_ylo, p_own, p_yhi)[dy + 1], 0, (r_ylo, r_own, r_yhi)[dy + 1], RADIUS_ROW)
        p_ref, r_ref = (p_xlo, r_xlo) if dx < 0 else (p_xhi, r_xhi)
        return p_ref, (dy + 1) * block, r_ref, (dy + 1) * 7 * L0 + RADIUS_ROW

    lane = lane_iota(8)
    tri_row = lax.broadcasted_iota(jnp.int32, (S, 2 * S), 0)
    tri_col = lax.broadcasted_iota(jnp.int32, (S, 2 * S), 1)
    tri = jnp.where((tri_row < tri_col) | (tri_col >= S), 1.0, 0.0).astype(jnp.bfloat16)

    for start in (0, 8, cells - 8):
        own_r = r_own[RADIUS_ROW + shift + start : RADIUS_ROW + shift + start + 8, :]
        own_live = own_r > 0.0
        bounds = []
        for f in range(3):
            first = f * layers + 1 + start
            value = p_own[first : first + 8, :]
            top = jnp.max(jnp.where(own_live, value, -FAR), axis=1, keepdims=True) + REACH
            bottom = jnp.min(jnp.where(own_live, value, FAR), axis=1, keepdims=True) - REACH
            bounds.append((jnp.broadcast_to(bottom, (8, S)), jnp.broadcast_to(top, (8, S))))
        used = jnp.max(
            jnp.where(own_live, (lane + 1).astype(jnp.float32), 0.0), axis=1, keepdims=True
        )
        for k, offset in enumerate(NEAR):
            p_ref, p_base, r_ref, r_base = source(offset[0], offset[1])
            row = r_base + shift + start + offset[2]
            keep = r_ref[row : row + 8, :] > least[offset[:2]]
            for f in range(3):
                row = p_base + f * layers + 1 + start + offset[2]
                value = p_ref[row : row + 8, :] + float(offset[f])
                keep = keep & (value >= bounds[f][0]) & (value <= bounds[f][1])
            mask_s[k * 8 : k * 8 + 8, :] = jnp.where(keep, 1.0, 0.0)
        pref_s[...] = jnp.dot(
            mask_s[...].astype(jnp.bfloat16), tri, preferred_element_type=jnp.float32
        )
        base = jnp.zeros((8, S), jnp.int32)
        for k, offset in enumerate(NEAR):
            before = pref_s[k * 8 : k * 8 + 8, 0:S].astype(jnp.int32)
            count = pref_s[k * 8 : k * 8 + 8, S : 2 * S].astype(jnp.int32)
            hop = jnp.where(mask_s[k * 8 : k * 8 + 8, :] > 0.0, lane - before, 0)
            for bit in range(7):
                step = 1 << bit
                moved = pltpu.roll(hop, S - step, 1)
                hop = jnp.where(
                    (moved & step) != 0, moved, jnp.where((hop & step) != 0, 0, hop)
                )
            slot = (lane - base) & (S - 1)
            pick = (jnp.take_along_axis(hop, slot, axis=1) + slot) & (S - 1)
            page = (base >> 7) + jnp.where(lane < (base & (S - 1)), 1, 0)
            key_s[k * 8 : k * 8 + 8, :] = jnp.where(slot < count, page, -1)
            base = base + count
            p_ref, p_base, r_ref, r_base = source(offset[0], offset[1])
            for f in range(7):
                if f < 6:
                    row = p_base + f * layers + 1 + start + offset[2]
                    value = p_ref[row : row + 8, :]
                    if f < 3 and offset[f] != 0:
                        value = value + float(offset[f])
                else:
                    row = r_base + shift + start + offset[2]
                    value = r_ref[row : row + 8, :]
                work_s[k, f] = jnp.take_along_axis(value, pick, axis=1)
        total = base.astype(jnp.float32)
        pages = (jnp.max(total).astype(jnp.int32) + (S - 1)) >> 7
        for i in range(8):
            rows_s[start + i] = (
                jnp.max(total[i : i + 1, :]).astype(jnp.int32) + (S - 1)
            ) >> 7
            slots_s[start + i] = jnp.max(used[i : i + 1, :]).astype(jnp.int32)

        def merge(page, carry):
            acc = [jnp.zeros((8, S), jnp.float32)] * 6 + [jnp.full((8, S), -10.0, jnp.float32)]
            for k in range(27):
                here = key_s[k * 8 : k * 8 + 8, :] == page
                acc = [jnp.where(here, work_s[k, f], acc[f]) for f in range(7)]
            for f in range(7):
                list_s[page, f, start : start + 8, :] = acc[f]
            return carry

        lax.fori_loop(0, pages, merge, 0)

    radius = r_own[RADIUS_ROW + shift : RADIUS_ROW + shift + cells, :]
    live = radius > 0.0
    own_s[...] = jnp.zeros(own_s.shape, jnp.float32)
    for f in range(7):
        value = (
            p_own[f * layers + 1 : f * layers + 1 + cells, :]
            if f < 6
            else jnp.where(live, radius, -10.0)
        )
        for part in range(3):
            piece = value.astype(jnp.bfloat16).astype(jnp.float32)
            own_s[pl.ds(part * 8 + f, cells, stride=32), :] = piece
            value = value - piece
    for i in range(cells):
        turn_s[i] = own_s[i * 32 : i * 32 + 32, :].T.astype(jnp.bfloat16)
    pick_row = lax.broadcasted_iota(jnp.int32, (32, 7 * S), 0)
    pick_col = lax.broadcasted_iota(jnp.int32, (32, 7 * S), 1)
    chosen = (pick_row < 24) & ((pick_row & 7) == (pick_col >> 7))
    pick_s[...] = jnp.where(chosen, 1.0, 0.0).astype(jnp.bfloat16)
    force_s[...] = jnp.zeros((S, S), jnp.float32)

    def spread_cell(cell, target):
        target[...] = jnp.dot(
            turn_s[cell], pick_s[...], preferred_element_type=jnp.float32
        )

    def near_page(cell, page, values, sums, tiles, fresh):
        near = [jnp.broadcast_to(list_s[page, f, pl.ds(cell, 1), :], (8, S)) for f in range(7)]
        for t in range(tiles):
            rows = slice(8 * t, 8 * t + 8)
            own = [values[rows, f * S : f * S + S] for f in range(7)]
            ex = near[0] - own[0]
            ey = near[1] - own[1]
            ez = near[2] - own[2]
            square = ex * ex + ey * ey + ez * ez + SOFTENING
            inverse = lax.rsqrt(square)
            press = jnp.maximum((near[6] + own[6]) - square * inverse, 0.0)
            closing = (
                (near[3] - own[3]) * ex + (near[4] - own[4]) * ey + (near[5] - own[5]) * ez
            )
            size = press * inverse * (1.0 - DAMPING * (closing * inverse))
            for f, part in enumerate((size * ex, size * ey, size * ez)):
                cols = slice(f * S, f * S + S)
                sums[rows, cols] = part if fresh else sums[rows, cols] + part

    def reduce_cell(cell, sums):
        for t in range(16):
            rows = slice(8 * t, 8 * t + 8)
            tile = force_s[rows, :]
            for f in range(3):
                total_f = jnp.sum(sums[rows, f * S : f * S + S], axis=1, keepdims=True)
                tile = jnp.where(
                    lane == f * 32 + cell, jnp.broadcast_to(total_f, (8, S)), tile
                )
            force_s[rows, :] = tile

    def one_cell(cell, values, next_values, sums, last_sums):
        spread_cell(jnp.minimum(cell + 1, cells - 1), next_values)
        reduce_cell(cell - 1, last_sums)
        near_page(cell, 0, values, sums, 16, True)
        few = slots_s[cell] <= 64
        page_count = rows_s[cell]

        def more(tiles):
            def step(page, carry):
                near_page(cell, page, values, sums, tiles, False)
                return carry

            lax.fori_loop(1, page_count, step, 0)

        @pl.when(few)
        def _():
            more(8)

        @pl.when(jnp.logical_not(few))
        def _():
            more(16)

    def two_cells(pair, carry):
        one_cell(2 * pair, cell_a, cell_b, acc_a, acc_b)
        one_cell(2 * pair + 1, cell_b, cell_a, acc_b, acc_a)
        return carry

    spread_cell(0, cell_a)
    lax.fori_loop(0, cells // 2, two_cells, 0)
    reduce_cell(cells - 1, acc_b)

    force = force_s[...].T
    scale = jnp.where(live, -1.0 / (radius * radius * radius), 0.0)
    for f in range(3):
        push = force[f * 32 : f * 32 + cells, :] * scale
        if f == 2:
            push = push - GRAVITY
        first = (3 + f) * layers + 1
        speed = p_own[first : first + cells, :] + TIME_STEP * push
        first = f * layers + 1
        place = p_own[first : first + cells, :] + TIME_STEP * speed
        out_ref[f * cells : f * cells + cells, :] = place
        out_ref[(3 + f) * cells : (3 + f) * cells + cells, :] = speed

    if deposit:
        dep_s, edge_s = rest[15:17]

        def one_deposit(cell):
            def row(f):
                return out_ref[pl.ds(f * cells + cell, 1), :]

            r = r_own[pl.ds(RADIUS_ROW + shift + cell, 1), :]
            volume = (4.0 * math.pi / 3.0 * B**3) * (r * r * r)
            plane = plane_weights(row(0), row(1))
            wz = axis_weights(row(2))
            carried = [volume, volume * row(3), volume * row(4), volume * row(5)]
            left = jnp.concatenate(
                [jnp.broadcast_to(c, (B, S)) * wz for c in carried], axis=0
            )
            return lax.dot_general(
                left,
                plane,
                (((1,), (1,)), ((), ())),
                precision=HIGHEST,
                preferred_element_type=jnp.float32,
            )

        def some_deposits(step, carry):
            blocks = [one_deposit(step * 3 + i) for i in range(3)]
            for i in range(3):
                for f in range(4):
                    dep_s[f, pl.ds(pl.multiple_of(step * 24 + i * 8, 8), 8), 0:64] = blocks[i][
                        f * 8 : f * 8 + 8, :
                    ]
            return carry

        lax.fori_loop(0, cells // 3, some_deposits, 0)
        edge_s[...] = jnp.zeros((S, S), jnp.float32)
        for f in range(4):
            edge_s[f * 32 : f * 32 + 8, :] = dep_s[f, B + S : B + S + 8, :]
            edge_s[f * 32 + 24 : f * 32 + 32, :] = dep_s[f, 0:B, :]
        for f in range(5):
            grid = (dep_s[f, B : B + S, :] if f < 4 else edge_s[...]).T
            dep_ref[f * 64 : f * 64 + 64, :] = grid[0:64, :]
            for x in range(B):
                row = (f * B + x) * WD
                dep_lo_ref[row : row + WD, :] = grid[x * B : x * B + WD, :]
                dep_hi_ref[row : row + WD, :] = grid[x * B + B - WD : x * B + B, :]


def pack_kernel(count_ref, pos_ref, vel_ref, rad_ref, gas_ref, prs_ref, out_ref):
    rank = lax.axis_index("gz")
    row = lax.broadcasted_iota(jnp.int32, (PZ, S), 0)
    counts = jnp.zeros((PZ, S), jnp.int32)
    for i in range(PZ):
        counts = jnp.where(row == i, count_ref[i], counts)
    live = lane_iota(PZ) < counts
    fields = [pos_ref[f * PZ : f * PZ + PZ, :] for f in range(3)]
    fields += [vel_ref[f * PZ : f * PZ + PZ, :] for f in range(3)]
    fields.append(jnp.where(live, rad_ref[...], 0.0))
    lower = rank >= PZ - 3
    for f in range(7):
        out_ref[pl.ds(f, PZ, stride=24), :] = fields[f]
        below = jnp.where(row == 0, 0.0, pltpu.roll(fields[f], 1, 0))
        above = jnp.where(row == PZ - 1, 0.0, pltpu.roll(fields[f], PZ - 1, 0))
        out_ref[pl.ds(7 + f, PZ, stride=24), :] = jnp.where(lower, below, above)
    first = gas_ref[0:S, :].T
    second = jnp.concatenate([gas_ref[S : S + 64, :], prs_ref[...]], axis=0).T
    for target in range(PZ):
        up = jnp.where(rank + 1 == target, 1.0, 0.0)
        down = jnp.where(rank - 1 == target, 1.0, 0.0)
        for i, turned in enumerate((first, second)):
            at = target * 24 + 14 + i * WG
            out_ref[at : at + WG, :] = turned[S - WG :, :] * up + turned[:WG, :] * down


def pack(*arrays):
    return pl.pallas_call(
        pack_kernel,
        out_shape=pltpu.VMEM((PZ * 24, S), jnp.float32),
        in_specs=[pl.BlockSpec(memory_space=pltpu.SMEM)]
        + [pl.BlockSpec(memory_space=pltpu.VMEM)] * 5,
        name="pack",
    )(*arrays)


def near(arrays):
    return [pltpu.with_memory_space_constraint(a, pltpu.VMEM) for a in arrays]


def contact(cells, deposit, places, radii):
    shapes = [pltpu.VMEM((6 * cells, S), jnp.float32)]
    scratch = [
        pltpu.VMEM((27 * 8, S), jnp.float32),
        pltpu.VMEM((27 * 8, 2 * S), jnp.float32),
        pltpu.VMEM((27, 7, 8, S), jnp.float32),
        pltpu.VMEM((27 * 8, S), jnp.int32),
        pltpu.VMEM((27, 7, 24, S), jnp.float32),
        pltpu.VMEM((5 * S, S), jnp.float32),
        pltpu.VMEM((L1, S, 32), jnp.bfloat16),
        pltpu.VMEM((32, 7 * S), jnp.bfloat16),
        pltpu.VMEM((S, 7 * S), jnp.float32),
        pltpu.VMEM((S, 7 * S), jnp.float32),
        pltpu.VMEM((S, 3 * S), jnp.float32),
        pltpu.VMEM((S, 3 * S), jnp.float32),
        pltpu.VMEM((S, S), jnp.float32),
        pltpu.SMEM((24,), jnp.int32),
        pltpu.SMEM((24,), jnp.int32),
    ]
    if deposit:
        shapes.append(pltpu.VMEM((5 * 64, S), jnp.float32))
        shapes += [pltpu.VMEM((5 * B * WD, S), jnp.float32)] * 2
        scratch += [pltpu.VMEM((4, S + 2 * B, S), jnp.float32), pltpu.VMEM((S, S), jnp.float32)]
    return pl.pallas_call(
        lambda *refs: contact_kernel(cells, deposit, *refs),
        out_shape=shapes,
        scratch_shapes=scratch,
        compiler_params=pltpu.CompilerParams(flags=FLAGS),
        name="contact_deposit" if deposit else "contact",
    )(*near(places), *near(radii))


def assemble(target, edge, own, ylo, yhi, xlo, xhi, y_at, x_at, width, weight):
    span = B + 2 * width

    def put(field, x, y, value):
        rows = slice(y, y + value.shape[0])
        if field < 4:
            target[field, x, rows, 0:S] = value
        else:
            edge[x, rows, :] = value

    for field in range(5):
        for x in range(B):
            row = (field * B + x) * B
            put(field, width + x, width, own[row : row + B, :])
            row = y_at + (field * B + x) * width
            put(field, width + x, 0, ylo[row : row + width, :] * weight[0, -1])
            put(field, width + x, width + B, yhi[row : row + width, :] * weight[0, 1])
        for x in range(width):
            for place, ref, side in ((x, xlo, -1), (width + B + x, xhi, 1)):
                row = x_at + (field * width + x) * B
                put(field, place, width, ref[row : row + B, :] * weight[side, 0])
                row = x_at + 5 * width * B + (field * width + x) * width
                put(field, place, 0, ref[row : row + width, :] * weight[side, -1])
                row += 5 * width * width
                put(field, place, width + B, ref[row : row + width, :] * weight[side, 1])
    lane = lane_iota(8)
    for field in range(4):
        index = field * 32 + jnp.where(
            lane < 64, jnp.minimum(lane, 15), jnp.maximum(lane - 96, 16)
        )
        for x in range(span):
            for y in range(0, edge.shape[1], 8):
                target[field, x, y : y + 8, S : 2 * S] = jnp.take_along_axis(
                    edge[x, y : y + 8, :], index, axis=1
                )


def gas_kernel(*refs):
    (
        g_own,
        g_ylo,
        g_yhi,
        g_xlo,
        g_xhi,
        d_own,
        d_ylo,
        d_yhi,
        d_xlo,
        d_xhi,
        state_ref,
        sent_ref,
        newv_ref,
        newp_ref,
        u_s,
        ue_s,
        d_s,
        de_s,
        flux_s,
        mid_s,
        inv_s,
        src_s,
        pa_s,
        pb_s,
        grad_s,
        field_s,
        pair_s,
        sum_s,
    ) = refs
    sides = has_sides()
    weight = {
        (dx, dy): jnp.where(sides[0][dx + 1] & sides[1][dy + 1], 1.0, 0.0)
        for dx in (-1, 0, 1)
        for dy in (-1, 0, 1)
    }
    assemble(u_s, ue_s, g_own, g_ylo, g_yhi, g_xlo, g_xhi, 0, 0, WG, weight)
    assemble(d_s, de_s, d_own, d_ylo, d_yhi, d_xlo, d_xhi, 0, 0, WD, weight)
    wide = B + 2 * WD
    ring = 2 * S

    def zdiff(value):
        return pltpu.roll(value, ring - 1, 1) - pltpu.roll(value, 1, 1)

    def zsum(value):
        return pltpu.roll(value, ring - 1, 1) + pltpu.roll(value, 1, 1)

    def ydiff(value):
        return pltpu.roll(value, wide - 1, 0) - pltpu.roll(value, 1, 0)

    def ysum(value):
        return pltpu.roll(value, wide - 1, 0) + pltpu.roll(value, 1, 0)

    for x in range(wide):
        speed = [u_s[d, x + 1, 1 : wide + 1, :] for d in range(3)]
        solids = d_s[0, x]
        voidage = 1.0 / (1.0 + solids)
        under = 1.0 / (voidage + GAS_STEP * GAS_DRAG * solids)
        inv_s[x] = 1.0 / (6.0 + voidage)
        for k in range(3):
            slope = speed[0] * (u_s[k, x + 2, 1 : wide + 1, :] - u_s[k, x, 1 : wide + 1, :])
            slope += speed[1] * (u_s[k, x + 1, 2 : wide + 2, :] - u_s[k, x + 1, 0:wide, :])
            slope += speed[2] * zdiff(speed[k])
            pulled = speed[k] - (0.5 * GAS_STEP) * slope
            middle = (voidage * pulled + GAS_STEP * GAS_DRAG * d_s[1 + k, x]) * under
            mid_s[k, x] = middle
            flux_s[k, x] = voidage * middle
        pa_s[x] = u_s[3, x + 1, 1 : wide + 1, :]
    for x in range(1, wide - 1):
        spread = (flux_s[0, x + 1] - flux_s[0, x - 1]) + ydiff(flux_s[1, x]) + zdiff(flux_s[2, x])
        src_s[x] = (-0.5 / GAS_STEP) * spread * inv_s[x]

    row = lax.broadcasted_iota(jnp.int32, (wide, ring), 0) - WD + lax.axis_index("gy") * B
    col = lax.broadcasted_iota(jnp.int32, (wide, ring), 1)
    col = jnp.where(col < ring - 64, col, col - ring) + lax.axis_index("gz") * S
    limits = (lax.axis_size("gx") * B, lax.axis_size("gy") * B, lax.axis_size("gz") * S)
    inside = (row >= 0) & (row < limits[1]) & (col >= 0) & (col < limits[2])
    for sweep in range(SWEEPS):
        old, new = (pa_s, pb_s) if sweep % 2 == 0 else (pb_s, pa_s)
        factor = chebyshev_factor(sweep, SWEEPS)
        for x in range(1 + sweep, wide - 1 - sweep):
            place = lax.axis_index("gx") * B + (x - WD)
            kept = jnp.where((place >= 0) & (place < limits[0]), 1.0, 0.0)
            middle = old[x]
            around = (old[x + 1] + old[x - 1]) + ysum(middle) + zsum(middle)
            value = middle + factor * (src_s[x] + around * inv_s[x] - middle)
            new[x] = jnp.where(inside, value, 0.0) * kept
    last = pb_s if SWEEPS % 2 == 1 else pa_s
    rows = slice(WD, WD + B)
    for x in range(B):
        plane = last[WD + x]
        slopes = (last[WD + x + 1] - last[WD + x - 1], ydiff(plane), zdiff(plane))
        newp_ref[x * B : x * B + B, :] = plane[rows, 0:S]
        for k in range(3):
            slope = 0.5 * slopes[k]
            at = (k * B + x) * B
            grad_s[at : at + B, :] = slope[rows, 0:S]
            newv_ref[at : at + B, :] = (mid_s[k, WD + x] - GAS_STEP * slope)[rows, 0:S]

    joined = (
        newv_ref[0:S, :],
        jnp.concatenate([newv_ref[S : S + 64, :], grad_s[0:64, :]], axis=0),
        grad_s[64:192, :],
    )
    for v in range(3):
        field_s[:, v * S : v * S + S] = joined[v].T
    pair_s[...] = jnp.zeros((4, S, 2 * S), jnp.float32)

    def some_cells(step, carry):
        for i in range(4):
            cell = step * 4 + i

            def row_of(f):
                return state_ref[pl.ds(f * L2 + 1 + cell, 1), :]

            plane_w = plane_weights(row_of(0), row_of(1))
            wz = axis_weights(row_of(2))
            pair_s[i, 0:64, 0:S] = plane_w
            pair_s[i, 64:S, S : 2 * S] = plane_w
            start = pl.multiple_of(cell * 8, 8)
            left = jnp.concatenate(
                [field_s[pl.ds(start, 8), v * S : v * S + S] for v in range(3)], axis=0
            )
            part = jnp.dot(
                left, pair_s[i], precision=HIGHEST, preferred_element_type=jnp.float32
            )
            for v in range(3):
                for odd in range(2):
                    value = part[v * 8 : v * 8 + 8, odd * S : odd * S + S] * wz
                    sum_s[pl.ds((2 * v + odd) * 16 + cell, 1), :] = jnp.sum(
                        value, axis=0, keepdims=True
                    )
        return carry

    lax.fori_loop(0, PZ // 4, some_cells, 0)
    for f in range(3):
        speed = state_ref[(3 + f) * L2 + 1 : (3 + f) * L2 + 17, :]
        gas = sum_s[f * 16 : f * 16 + 16, :]
        slope = sum_s[(3 + f) * 16 : (3 + f) * 16 + 16, :]
        sent_ref[pl.ds(f, PZ, stride=8), :] = state_ref[f * L2 + 1 : f * L2 + 17, :]
        sent_ref[pl.ds(3 + f, PZ, stride=8), :] = (
            speed + COUPLE_STEP * (PARTICLE_DRAG * gas - slope)
        ) / (1.0 + COUPLE_STEP * PARTICLE_DRAG)


def gas_and_sample(gas, deposits, state):
    wide = B + 2 * WD
    ring = 2 * S
    return pl.pallas_call(
        gas_kernel,
        out_shape=[
            pltpu.VMEM((PZ * 8, S), jnp.float32),
            jax.ShapeDtypeStruct((3 * 64, S), jnp.float32),
            jax.ShapeDtypeStruct((64, S), jnp.float32),
        ],
        scratch_shapes=[
            pltpu.VMEM((4, B + 2 * WG, 24, ring), jnp.float32),
            pltpu.VMEM((B + 2 * WG, 24, S), jnp.float32),
            pltpu.VMEM((4, wide, wide, ring), jnp.float32),
            pltpu.VMEM((wide, wide, S), jnp.float32),
            pltpu.VMEM((3, wide, wide, ring), jnp.float32),
            pltpu.VMEM((3, wide, wide, ring), jnp.float32),
            pltpu.VMEM((wide, wide, ring), jnp.float32),
            pltpu.VMEM((wide, wide, ring), jnp.float32),
            pltpu.VMEM((wide, wide, ring), jnp.float32),
            pltpu.VMEM((wide, wide, ring), jnp.float32),
            pltpu.VMEM((3 * 64, S), jnp.float32),
            pltpu.VMEM((S, 3 * S), jnp.float32),
            pltpu.VMEM((4, S, 2 * S), jnp.float32),
            pltpu.VMEM((96, S), jnp.float32),
        ],
        name="gas_sample",
    )(*near((*gas, *deposits, state)))


def body(position, velocity, radius, cell_count, gas_velocity, pressure):
    rank = lax.axis_index("gz")
    count = lax.axis_size("gz")
    gas = jnp.concatenate([gas_velocity, pressure[None]], axis=0)
    sent = pack(
        cell_count.reshape(PZ),
        position.reshape(3 * PZ, S),
        velocity.reshape(3 * PZ, S),
        radius.reshape(PZ, S),
        gas_velocity.reshape(3 * B * B, S),
        pressure.reshape(B * B, S),
    )
    got = lax.all_to_all(sent, "gz", split_axis=0, concat_axis=0, tiled=True)
    got = got.reshape(PZ, 24, S)
    layers = jnp.concatenate([got[PZ - 3 :, 7:14], got[:, :7], got[:3, 7:14]], axis=0)
    own = jnp.swapaxes(layers, 0, 1).reshape(7 * L0, S)
    from_low = lax.dynamic_index_in_dim(got, jnp.maximum(rank - 1, 0), 0, keepdims=False)
    from_high = lax.dynamic_index_in_dim(got, jnp.minimum(rank + 1, count - 1), 0, keepdims=False)
    def edge(rows, there):
        rows = jnp.where(there, rows[14:], 0.0).reshape(2, WG, 2, B * B)
        return jnp.transpose(rows, (0, 2, 3, 1)).reshape(4, B * B, WG)

    zlo = edge(from_low, rank > 0)
    zhi = edge(from_high, rank < count - 1)
    packed = jnp.concatenate([zhi, jnp.zeros((4, B * B, 32 - 2 * WG), jnp.float32), zlo], axis=2)
    packed = jnp.swapaxes(packed, 0, 1).reshape(B * B, S)
    gas5 = jnp.concatenate([gas.reshape(4 * B * B, S), packed], axis=0)

    def y_slab(first):
        return gas5.reshape(5, B, B, S)[:, :, first : first + WG].reshape(5 * B * WG, S)

    def x_slab(ylo, yhi, first, at, width, block):
        parts = [block.reshape(5, B, B * S)[:, first : first + width].reshape(-1, S)]
        for part in (ylo, yhi):
            part = part[at:].reshape(5, B, width * S)[:, first : first + width]
            parts.append(part.reshape(-1, S))
        return parts

    ylo, yhi = shift_pair(own, own, "gy")
    column = jnp.concatenate([ylo, own, yhi], axis=0)
    xlo, xhi = shift_pair(column, column, "gx")
    first = (own, ylo, yhi, xlo, xhi)
    (moved,) = contact(L1, False, first, first)

    gylo, gyhi = shift_pair(y_slab(0), y_slab(B - WG), "gy")
    ylo, yhi = shift_pair(moved, moved, "gy")
    gxlo, gxhi = shift_pair(
        jnp.concatenate(x_slab(gylo, gyhi, 0, 0, WG, gas5), axis=0),
        jnp.concatenate(x_slab(gylo, gyhi, B - WG, 0, WG, gas5), axis=0),
        "gx",
    )
    column = jnp.concatenate([ylo, moved, yhi], axis=0)
    xlo, xhi = shift_pair(column, column, "gx")
    final, dep, dep_low, dep_high = contact(L2, True, (moved, ylo, yhi, xlo, xhi), first)

    dylo, dyhi = shift_pair(dep_low, dep_high, "gy")
    dxlo, dxhi = shift_pair(
        jnp.concatenate(x_slab(dylo, dyhi, 0, 0, WD, dep), axis=0),
        jnp.concatenate(x_slab(dylo, dyhi, B - WD, 0, WD, dep), axis=0),
        "gx",
    )
    sent_back, new_velocity, new_pressure = gas_and_sample(
        (gas5, gylo, gyhi, gxlo, gxhi), (dep, dylo, dyhi, dxlo, dxhi), final
    )
    returned = lax.all_to_all(sent_back, "gz", split_axis=0, concat_axis=0, tiled=True)
    returned = jnp.swapaxes(returned.reshape(PZ, 8, S)[:, :6], 0, 1)[:, None, None]
    return (
        returned[:3],
        returned[3:],
        new_velocity.reshape(3, B, B, S),
        new_pressure.reshape(B, B, S),
    )


def solution(mesh):
    placed = (
        P(None, "gx", "gy", "gz", None),
        P(None, "gx", "gy", "gz", None),
        P("gx", "gy", "gz", None),
        P("gx", "gy", "gz"),
        P(None, "gx", "gy", "gz"),
        P("gx", "gy", "gz"),
    )
    return jax.shard_map(
        body,
        mesh=mesh,
        in_specs=placed,
        out_specs=(
            P(None, "gx", "gy", "gz", None),
            P(None, "gx", "gy", "gz", None),
            P(None, "gx", "gy", "gz"),
            P("gx", "gy", "gz"),
        ),
        check_vma=False,
    )
```

```python
import math

import jax
import jax.numpy as jnp
from jax import lax
from jax.experimental import pallas as pl
from jax.experimental.pallas import tpu as pltpu
from jax.sharding import PartitionSpec as P

B = 8
S = 128
PZ = 16
SWEEPS = 3
DAMPING = 0.5
TIME_STEP = 0.005
GRAVITY = 1.0
SOFTENING = 0.0025
GAS_STEP = 0.2
GAS_DRAG = 2.0
PARTICLE_DRAG = 4.0
COUPLE_STEP = 0.25
LOWER_BOUND = 0.2
UPPER_BOUND = 2.0

REACH = 0.194
FAR = 1e30
NEAR = tuple((dx, dy, dz) for dx in (-1, 0, 1) for dy in (-1, 0, 1) for dz in (-1, 0, 1))
HIGHEST = lax.Precision.HIGHEST
FLAGS = {}

L0 = PZ + 6
L1 = PZ + 4
L2 = PZ + 2
RADIUS_ROW = 6 * L0
WG = 5
WD = 4


def shift_pair(array_low, array_high, axis):
    count = lax.axis_size(axis)
    forward = [(i, (i + 1) % count) for i in range(count)]
    backward = [((i + 1) % count, i) for i in range(count)]
    from_below = lax.ppermute(array_high, axis, forward)
    from_above = lax.ppermute(array_low, axis, backward)
    return from_below, from_above


def chebyshev_factor(sweep_index, sweeps):
    centre = 0.5 * (UPPER_BOUND + LOWER_BOUND)
    radius_half = 0.5 * (UPPER_BOUND - LOWER_BOUND)
    return 1.0 / (centre + radius_half * math.cos(math.pi * (2 * sweep_index + 1) / (2 * sweeps)))


def has_sides():
    ranks = [lax.axis_index(axis) for axis in ("gx", "gy")]
    sizes = [lax.axis_size(axis) for axis in ("gx", "gy")]
    return tuple((r > 0, r >= 0, r < n - 1) for r, n in zip(ranks, sizes))


def lane_iota(rows):
    return lax.broadcasted_iota(jnp.int32, (rows, S), 1)


def axis_weights(row):
    centres = lax.broadcasted_iota(jnp.int32, (B, S), 0).astype(jnp.float32) + 0.5
    gap = jnp.broadcast_to(row, (B, S)) * float(B) - centres
    kernel = jnp.exp(-gap * gap)
    return kernel / jnp.sum(kernel, axis=0, keepdims=True)


def plane_weights(row_x, row_y):
    wx = axis_weights(row_x)
    wy = axis_weights(row_y)
    return jnp.concatenate(
        [jnp.broadcast_to(wx[a : a + 1], (B, S)) * wy for a in range(B)], axis=0
    )


def contact_kernel(cells, deposit, *refs):
    p_own, p_ylo, p_yhi, p_xlo, p_xhi, r_own, r_ylo, r_yhi, r_xlo, r_xhi = refs[:10]
    out_ref = refs[10]
    rest = refs[11:]
    if deposit:
        dep_ref, dep_lo_ref, dep_hi_ref = rest[:3]
        rest = rest[3:]
    mask_s, pref_s, work_s, key_s, list_s, own_s, turn_s, pick_s = rest[:8]
    cell_a, cell_b, acc_a, acc_b, force_s, rows_s, slots_s = rest[8:15]
    sides = has_sides()
    least = {
        (dx, dy): jnp.where(sides[0][dx + 1] & sides[1][dy + 1], 0.0, FAR)
        for dx in (-1, 0, 1)
        for dy in (-1, 0, 1)
    }
    layers = cells + 2
    shift = (L0 - cells) // 2
    block = 7 * L0 if cells == L1 else 6 * L1

    def source(dx, dy):
        if dx == 0:
            return ((p_ylo, p_own, p_yhi)[dy + 1], 0, (r_ylo, r_own, r_yhi)[dy + 1], RADIUS_ROW)
        p_ref, r_ref = (p_xlo, r_xlo) if dx < 0 else (p_xhi, r_xhi)
        return p_ref, (dy + 1) * block, r_ref, (dy + 1) * 7 * L0 + RADIUS_ROW

    lane = lane_iota(8)
    tri_row = lax.broadcasted_iota(jnp.int32, (S, 2 * S), 0)
    tri_col = lax.broadcasted_iota(jnp.int32, (S, 2 * S), 1)
    tri = jnp.where((tri_row < tri_col) | (tri_col >= S), 1.0, 0.0).astype(jnp.bfloat16)

    for start in (0, 8, cells - 8):
        own_r = r_own[RADIUS_ROW + shift + start : RADIUS_ROW + shift + start + 8, :]
        own_live = own_r > 0.0
        bounds = []
        for f in range(3):
            first = f * layers + 1 + start
            value = p_own[first : first + 8, :]
            top = jnp.max(jnp.where(own_live, value, -FAR), axis=1, keepdims=True) + REACH
            bottom = jnp.min(jnp.where(own_live, value, FAR), axis=1, keepdims=True) - REACH
            bounds.append((jnp.broadcast_to(bottom, (8, S)), jnp.broadcast_to(top, (8, S))))
        used = jnp.max(
            jnp.where(own_live, (lane + 1).astype(jnp.float32), 0.0), axis=1, keepdims=True
        )
        for k, offset in enumerate(NEAR):
            p_ref, p_base, r_ref, r_base = source(offset[0], offset[1])
            row = r_base + shift + start + offset[2]
            keep = r_ref[row : row + 8, :] > least[offset[:2]]
            for f in range(3):
                row = p_base + f * layers + 1 + start + offset[2]
                value = p_ref[row : row + 8, :] + float(offset[f])
                keep = keep & (value >= bounds[f][0]) & (value <= bounds[f][1])
            mask_s[k * 8 : k * 8 + 8, :] = jnp.where(keep, 1.0, 0.0)
        pref_s[...] = jnp.dot(
            mask_s[...].astype(jnp.bfloat16), tri, preferred_element_type=jnp.float32
        )
        base = jnp.zeros((8, S), jnp.int32)
        for k, offset in enumerate(NEAR):
            before = pref_s[k * 8 : k * 8 + 8, 0:S].astype(jnp.int32)
            count = pref_s[k * 8 : k * 8 + 8, S : 2 * S].astype(jnp.int32)
            hop = jnp.where(mask_s[k * 8 : k * 8 + 8, :] > 0.0, lane - before, 0)
            for bit in range(7):
                step = 1 << bit
                moved = pltpu.roll(hop, S - step, 1)
                hop = jnp.where(
                    (moved & step) != 0, moved, jnp.where((hop & step) != 0, 0, hop)
                )
            slot = (lane - base) & (S - 1)
            pick = (jnp.take_along_axis(hop, slot, axis=1) + slot) & (S - 1)
            page = (base >> 7) + jnp.where(lane < (base & (S - 1)), 1, 0)
            key_s[k * 8 : k * 8 + 8, :] = jnp.where(slot < count, page, -1)
            base = base + count
            p_ref, p_base, r_ref, r_base = source(offset[0], offset[1])
            for f in range(7):
                if f < 6:
                    row = p_base + f * layers + 1 + start + offset[2]
                    value = p_ref[row : row + 8, :]
                    if f < 3 and offset[f] != 0:
                        value = value + float(offset[f])
                else:
                    row = r_base + shift + start + offset[2]
                    value = r_ref[row : row + 8, :]
                work_s[k, f] = jnp.take_along_axis(value, pick, axis=1)
        total = base.astype(jnp.float32)
        pages = (jnp.max(total).astype(jnp.int32) + (S - 1)) >> 7
        for i in range(8):
            rows_s[start + i] = (
                jnp.max(total[i : i + 1, :]).astype(jnp.int32) + (S - 1)
            ) >> 7
            slots_s[start + i] = jnp.max(used[i : i + 1, :]).astype(jnp.int32)

        def merge(page, carry):
            acc = [jnp.zeros((8, S), jnp.float32)] * 6 + [jnp.full((8, S), -10.0, jnp.float32)]
            for k in range(27):
                here = key_s[k * 8 : k * 8 + 8, :] == page
                acc = [jnp.where(here, work_s[k, f], acc[f]) for f in range(7)]
            for f in range(7):
                list_s[page, f, start : start + 8, :] = acc[f]
            return carry

        lax.fori_loop(0, pages, merge, 0)

    radius = r_own[RADIUS_ROW + shift : RADIUS_ROW + shift + cells, :]
    live = radius > 0.0
    own_s[...] = jnp.zeros(own_s.shape, jnp.float32)
    for f in range(7):
        value = (
            p_own[f * layers + 1 : f * layers + 1 + cells, :]
            if f < 6
            else jnp.where(live, radius, -10.0)
        )
        for part in range(3):
            piece = value.astype(jnp.bfloat16).astype(jnp.float32)
            own_s[pl.ds(part * 8 + f, cells, stride=32), :] = piece
            value = value - piece
    for i in range(cells):
        turn_s[i] = own_s[i * 32 : i * 32 + 32, :].T.astype(jnp.bfloat16)
    pick_row = lax.broadcasted_iota(jnp.int32, (32, 7 * S), 0)
    pick_col = lax.broadcasted_iota(jnp.int32, (32, 7 * S), 1)
    chosen = (pick_row < 24) & ((pick_row & 7) == (pick_col >> 7))
    pick_s[...] = jnp.where(chosen, 1.0, 0.0).astype(jnp.bfloat16)
    force_s[...] = jnp.zeros((S, S), jnp.float32)

    def spread_cell(cell, target):
        target[...] = jnp.dot(
            turn_s[cell], pick_s[...], preferred_element_type=jnp.float32
        )

    def near_pages(cell, pages, values, sums, tiles, fresh):
        lists = [
            [jnp.broadcast_to(list_s[page, f, pl.ds(cell, 1), :], (8, S)) for f in range(7)]
            for page in pages
        ]
        for t in range(tiles):
            rows = slice(8 * t, 8 * t + 8)
            own = [values[rows, f * S : f * S + S] for f in range(7)]
            total = None
            for near in lists:
                part = pair_force(near, own)
                total = part if total is None else [a + b for a, b in zip(total, part)]
            for f in range(3):
                cols = slice(f * S, f * S + S)
                sums[rows, cols] = total[f] if fresh else sums[rows, cols] + total[f]

    def pair_force(near, own):
        ex = near[0] - own[0]
        ey = near[1] - own[1]
        ez = near[2] - own[2]
        square = ex * ex + ey * ey + ez * ez + SOFTENING
        inverse = lax.rsqrt(square)
        press = jnp.maximum((near[6] + own[6]) - square * inverse, 0.0)
        closing = (
            (near[3] - own[3]) * ex + (near[4] - own[4]) * ey + (near[5] - own[5]) * ez
        )
        size = press * inverse * (1.0 - DAMPING * (closing * inverse))
        return size * ex, size * ey, size * ez

    def reduce_cell(cell, sums):
        for t in range(16):
            rows = slice(8 * t, 8 * t + 8)
            tile = force_s[rows, :]
            for f in range(3):
                total_f = jnp.sum(sums[rows, f * S : f * S + S], axis=1, keepdims=True)
                tile = jnp.where(
                    lane == f * 32 + cell, jnp.broadcast_to(total_f, (8, S)), tile
                )
            force_s[rows, :] = tile

    def one_cell(cell, values, next_values, sums, last_sums):
        spread_cell(jnp.minimum(cell + 1, cells - 1), next_values)
        reduce_cell(cell - 1, last_sums)
        near_pages(cell, (0,), values, sums, 16, True)
        few = slots_s[cell] <= 64
        page_count = rows_s[cell]

        def more(tiles):
            def step(pair, carry):
                pages = (2 * pair - 1, 2 * pair)
                near_pages(cell, pages, values, sums, tiles, False)
                return carry

            lax.fori_loop(1, (page_count + 1) >> 1, step, 0)

            @pl.when((page_count > 1) & ((page_count & 1) == 0))
            def _():
                near_pages(cell, (page_count - 1,), values, sums, tiles, False)

        @pl.when(few)
        def _():
            more(8)

        @pl.when(jnp.logical_not(few))
        def _():
            more(16)

    def two_cells(pair, carry):
        one_cell(2 * pair, cell_a, cell_b, acc_a, acc_b)
        one_cell(2 * pair + 1, cell_b, cell_a, acc_b, acc_a)
        return carry

    spread_cell(0, cell_a)
    lax.fori_loop(0, cells // 2, two_cells, 0)
    reduce_cell(cells - 1, acc_b)

    force = force_s[...].T
    scale = jnp.where(live, -1.0 / (radius * radius * radius), 0.0)
    for f in range(3):
        push = force[f * 32 : f * 32 + cells, :] * scale
        if f == 2:
            push = push - GRAVITY
        first = (3 + f) * layers + 1
        speed = p_own[first : first + cells, :] + TIME_STEP * push
        first = f * layers + 1
        place = p_own[first : first + cells, :] + TIME_STEP * speed
        out_ref[f * cells : f * cells + cells, :] = place
        out_ref[(3 + f) * cells : (3 + f) * cells + cells, :] = speed

    if deposit:
        dep_s, edge_s = rest[15:17]

        def one_deposit(cell):
            def row(f):
                return out_ref[pl.ds(f * cells + cell, 1), :]

            r = r_own[pl.ds(RADIUS_ROW + shift + cell, 1), :]
            volume = (4.0 * math.pi / 3.0 * B**3) * (r * r * r)
            plane = plane_weights(row(0), row(1))
            wz = axis_weights(row(2))
            carried = [volume, volume * row(3), volume * row(4), volume * row(5)]
            left = jnp.concatenate(
                [jnp.broadcast_to(c, (B, S)) * wz for c in carried], axis=0
            )
            return lax.dot_general(
                left,
                plane,
                (((1,), (1,)), ((), ())),
                precision=HIGHEST,
                preferred_element_type=jnp.float32,
            )

        def some_deposits(step, carry):
            blocks = [one_deposit(step * 3 + i) for i in range(3)]
            for i in range(3):
                for f in range(4):
                    dep_s[f, pl.ds(pl.multiple_of(step * 24 + i * 8, 8), 8), 0:64] = blocks[i][
                        f * 8 : f * 8 + 8, :
                    ]
            return carry

        lax.fori_loop(0, cells // 3, some_deposits, 0)
        edge_s[...] = jnp.zeros((S, S), jnp.float32)
        for f in range(4):
            edge_s[f * 32 : f * 32 + 8, :] = dep_s[f, B + S : B + S + 8, :]
            edge_s[f * 32 + 24 : f * 32 + 32, :] = dep_s[f, 0:B, :]
        for f in range(5):
            grid = (dep_s[f, B : B + S, :] if f < 4 else edge_s[...]).T
            dep_ref[f * 64 : f * 64 + 64, :] = grid[0:64, :]
            for x in range(B):
                row = (f * B + x) * WD
                dep_lo_ref[row : row + WD, :] = grid[x * B : x * B + WD, :]
                dep_hi_ref[row : row + WD, :] = grid[x * B + B - WD : x * B + B, :]


def pack_kernel(count_ref, pos_ref, vel_ref, rad_ref, gas_ref, prs_ref, out_ref):
    rank = lax.axis_index("gz")
    row = lax.broadcasted_iota(jnp.int32, (PZ, S), 0)
    counts = jnp.zeros((PZ, S), jnp.int32)
    for i in range(PZ):
        counts = jnp.where(row == i, count_ref[i], counts)
    live = lane_iota(PZ) < counts
    fields = [pos_ref[f * PZ : f * PZ + PZ, :] for f in range(3)]
    fields += [vel_ref[f * PZ : f * PZ + PZ, :] for f in range(3)]
    fields.append(jnp.where(live, rad_ref[...], 0.0))
    lower = rank >= PZ - 3
    for f in range(7):
        out_ref[pl.ds(f, PZ, stride=24), :] = fields[f]
        below = jnp.where(row == 0, 0.0, pltpu.roll(fields[f], 1, 0))
        above = jnp.where(row == PZ - 1, 0.0, pltpu.roll(fields[f], PZ - 1, 0))
        out_ref[pl.ds(7 + f, PZ, stride=24), :] = jnp.where(lower, below, above)
    first = gas_ref[0:S, :].T
    second = jnp.concatenate([gas_ref[S : S + 64, :], prs_ref[...]], axis=0).T
    for target in range(PZ):
        up = jnp.where(rank + 1 == target, 1.0, 0.0)
        down = jnp.where(rank - 1 == target, 1.0, 0.0)
        for i, turned in enumerate((first, second)):
            at = target * 24 + 14 + i * WG
            out_ref[at : at + WG, :] = turned[S - WG :, :] * up + turned[:WG, :] * down


def pack(*arrays):
    return pl.pallas_call(
        pack_kernel,
        out_shape=pltpu.VMEM((PZ * 24, S), jnp.float32),
        in_specs=[pl.BlockSpec(memory_space=pltpu.SMEM)]
        + [pl.BlockSpec(memory_space=pltpu.VMEM)] * 5,
        name="pack",
    )(*arrays)


def unpack_kernel(got_ref, place_ref, speed_ref):
    for f in range(3):
        place_ref[f * PZ : f * PZ + PZ, :] = got_ref[pl.ds(f, PZ, stride=8), :]
        speed_ref[f * PZ : f * PZ + PZ, :] = got_ref[pl.ds(3 + f, PZ, stride=8), :]


def unpack(got):
    return pl.pallas_call(
        unpack_kernel,
        out_shape=[jax.ShapeDtypeStruct((3 * PZ, S), jnp.float32)] * 2,
        name="unpack",
    )(*near([got]))


def near(arrays):
    return [pltpu.with_memory_space_constraint(a, pltpu.VMEM) for a in arrays]


def contact(cells, deposit, places, radii):
    shapes = [pltpu.VMEM((6 * cells, S), jnp.float32)]
    scratch = [
        pltpu.VMEM((27 * 8, S), jnp.float32),
        pltpu.VMEM((27 * 8, 2 * S), jnp.float32),
        pltpu.VMEM((27, 7, 8, S), jnp.float32),
        pltpu.VMEM((27 * 8, S), jnp.int32),
        pltpu.VMEM((27, 7, 24, S), jnp.float32),
        pltpu.VMEM((5 * S, S), jnp.float32),
        pltpu.VMEM((L1, S, 32), jnp.bfloat16),
        pltpu.VMEM((32, 7 * S), jnp.bfloat16),
        pltpu.VMEM((S, 7 * S), jnp.float32),
        pltpu.VMEM((S, 7 * S), jnp.float32),
        pltpu.VMEM((S, 3 * S), jnp.float32),
        pltpu.VMEM((S, 3 * S), jnp.float32),
        pltpu.VMEM((S, S), jnp.float32),
        pltpu.SMEM((24,), jnp.int32),
        pltpu.SMEM((24,), jnp.int32),
    ]
    if deposit:
        shapes.append(pltpu.VMEM((5 * 64, S), jnp.float32))
        shapes += [pltpu.VMEM((5 * B * WD, S), jnp.float32)] * 2
        scratch += [pltpu.VMEM((4, S + 2 * B, S), jnp.float32), pltpu.VMEM((S, S), jnp.float32)]
    return pl.pallas_call(
        lambda *refs: contact_kernel(cells, deposit, *refs),
        out_shape=shapes,
        scratch_shapes=scratch,
        compiler_params=pltpu.CompilerParams(flags=FLAGS),
        name="contact_deposit" if deposit else "contact",
    )(*near(places), *near(radii))


def assemble(target, edge, own, ylo, yhi, xlo, xhi, y_at, x_at, width, weight):
    span = B + 2 * width

    def put(field, x, y, value):
        rows = slice(y, y + value.shape[0])
        if field < 4:
            target[field, x, rows, 0:S] = value
        else:
            edge[x, rows, :] = value

    for field in range(5):
        for x in range(B):
            row = (field * B + x) * B
            put(field, width + x, width, own[row : row + B, :])
            row = y_at + (field * B + x) * width
            put(field, width + x, 0, ylo[row : row + width, :] * weight[0, -1])
            put(field, width + x, width + B, yhi[row : row + width, :] * weight[0, 1])
        for x in range(width):
            for place, ref, side in ((x, xlo, -1), (width + B + x, xhi, 1)):
                row = x_at + (field * width + x) * B
                put(field, place, width, ref[row : row + B, :] * weight[side, 0])
                row = x_at + 5 * width * B + (field * width + x) * width
                put(field, place, 0, ref[row : row + width, :] * weight[side, -1])
                row += 5 * width * width
                put(field, place, width + B, ref[row : row + width, :] * weight[side, 1])
    lane = lane_iota(8)
    for field in range(4):
        index = field * 32 + jnp.where(
            lane < 64, jnp.minimum(lane, 15), jnp.maximum(lane - 96, 16)
        )
        for x in range(span):
            for y in range(0, edge.shape[1], 8):
                target[field, x, y : y + 8, S : 2 * S] = jnp.take_along_axis(
                    edge[x, y : y + 8, :], index, axis=1
                )


def gas_kernel(*refs):
    (
        g_own,
        g_ylo,
        g_yhi,
        g_xlo,
        g_xhi,
        d_own,
        d_ylo,
        d_yhi,
        d_xlo,
        d_xhi,
        state_ref,
        sent_ref,
        newv_ref,
        newp_ref,
        u_s,
        ue_s,
        d_s,
        de_s,
        flux_s,
        mid_s,
        inv_s,
        src_s,
        pa_s,
        pb_s,
        grad_s,
        field_s,
        pair_s,
        sum_s,
    ) = refs
    sides = has_sides()
    weight = {
        (dx, dy): jnp.where(sides[0][dx + 1] & sides[1][dy + 1], 1.0, 0.0)
        for dx in (-1, 0, 1)
        for dy in (-1, 0, 1)
    }
    assemble(u_s, ue_s, g_own, g_ylo, g_yhi, g_xlo, g_xhi, 0, 0, WG, weight)
    assemble(d_s, de_s, d_own, d_ylo, d_yhi, d_xlo, d_xhi, 0, 0, WD, weight)
    wide = B + 2 * WD
    ring = 2 * S

    def zdiff(value):
        return pltpu.roll(value, ring - 1, 1) - pltpu.roll(value, 1, 1)

    def zsum(value):
        return pltpu.roll(value, ring - 1, 1) + pltpu.roll(value, 1, 1)

    def ydiff(value):
        return pltpu.roll(value, wide - 1, 0) - pltpu.roll(value, 1, 0)

    def ysum(value):
        return pltpu.roll(value, wide - 1, 0) + pltpu.roll(value, 1, 0)

    for x in range(wide):
        speed = [u_s[d, x + 1, 1 : wide + 1, :] for d in range(3)]
        solids = d_s[0, x]
        voidage = 1.0 / (1.0 + solids)
        under = 1.0 / (voidage + GAS_STEP * GAS_DRAG * solids)
        inv_s[x] = 1.0 / (6.0 + voidage)
        for k in range(3):
            slope = speed[0] * (u_s[k, x + 2, 1 : wide + 1, :] - u_s[k, x, 1 : wide + 1, :])
            slope += speed[1] * (u_s[k, x + 1, 2 : wide + 2, :] - u_s[k, x + 1, 0:wide, :])
            slope += speed[2] * zdiff(speed[k])
            pulled = speed[k] - (0.5 * GAS_STEP) * slope
            middle = (voidage * pulled + GAS_STEP * GAS_DRAG * d_s[1 + k, x]) * under
            mid_s[k, x] = middle
            flux_s[k, x] = voidage * middle
        pa_s[x] = u_s[3, x + 1, 1 : wide + 1, :]
    for x in range(1, wide - 1):
        spread = (flux_s[0, x + 1] - flux_s[0, x - 1]) + ydiff(flux_s[1, x]) + zdiff(flux_s[2, x])
        src_s[x] = (-0.5 / GAS_STEP) * spread * inv_s[x]

    row = lax.broadcasted_iota(jnp.int32, (wide, ring), 0) - WD + lax.axis_index("gy") * B
    col = lax.broadcasted_iota(jnp.int32, (wide, ring), 1)
    col = jnp.where(col < ring - 64, col, col - ring) + lax.axis_index("gz") * S
    limits = (lax.axis_size("gx") * B, lax.axis_size("gy") * B, lax.axis_size("gz") * S)
    inside = (row >= 0) & (row < limits[1]) & (col >= 0) & (col < limits[2])
    for sweep in range(SWEEPS):
        old, new = (pa_s, pb_s) if sweep % 2 == 0 else (pb_s, pa_s)
        factor = chebyshev_factor(sweep, SWEEPS)
        for x in range(1 + sweep, wide - 1 - sweep):
            place = lax.axis_index("gx") * B + (x - WD)
            kept = jnp.where((place >= 0) & (place < limits[0]), 1.0, 0.0)
            middle = old[x]
            around = (old[x + 1] + old[x - 1]) + ysum(middle) + zsum(middle)
            value = middle + factor * (src_s[x] + around * inv_s[x] - middle)
            new[x] = jnp.where(inside, value, 0.0) * kept
    last = pb_s if SWEEPS % 2 == 1 else pa_s
    rows = slice(WD, WD + B)
    for x in range(B):
        plane = last[WD + x]
        slopes = (last[WD + x + 1] - last[WD + x - 1], ydiff(plane), zdiff(plane))
        newp_ref[x * B : x * B + B, :] = plane[rows, 0:S]
        for k in range(3):
            slope = 0.5 * slopes[k]
            at = (k * B + x) * B
            grad_s[at : at + B, :] = slope[rows, 0:S]
            newv_ref[at : at + B, :] = (mid_s[k, WD + x] - GAS_STEP * slope)[rows, 0:S]

    joined = (
        newv_ref[0:S, :],
        jnp.concatenate([newv_ref[S : S + 64, :], grad_s[0:64, :]], axis=0),
        grad_s[64:192, :],
    )
    for v in range(3):
        field_s[:, v * S : v * S + S] = joined[v].T
    pair_s[...] = jnp.zeros((4, S, 2 * S), jnp.float32)

    def some_cells(step, carry):
        for i in range(4):
            cell = step * 4 + i

            def row_of(f):
                return state_ref[pl.ds(f * L2 + 1 + cell, 1), :]

            plane_w = plane_weights(row_of(0), row_of(1))
            wz = axis_weights(row_of(2))
            pair_s[i, 0:64, 0:S] = plane_w
            pair_s[i, 64:S, S : 2 * S] = plane_w
            start = pl.multiple_of(cell * 8, 8)
            left = jnp.concatenate(
                [field_s[pl.ds(start, 8), v * S : v * S + S] for v in range(3)], axis=0
            )
            part = jnp.dot(
                left, pair_s[i], precision=HIGHEST, preferred_element_type=jnp.float32
            )
            for v in range(3):
                for odd in range(2):
                    value = part[v * 8 : v * 8 + 8, odd * S : odd * S + S] * wz
                    sum_s[pl.ds((2 * v + odd) * 16 + cell, 1), :] = jnp.sum(
                        value, axis=0, keepdims=True
                    )
        return carry

    lax.fori_loop(0, PZ // 4, some_cells, 0)
    for f in range(3):
        speed = state_ref[(3 + f) * L2 + 1 : (3 + f) * L2 + 17, :]
        gas = sum_s[f * 16 : f * 16 + 16, :]
        slope = sum_s[(3 + f) * 16 : (3 + f) * 16 + 16, :]
        sent_ref[pl.ds(f, PZ, stride=8), :] = state_ref[f * L2 + 1 : f * L2 + 17, :]
        sent_ref[pl.ds(3 + f, PZ, stride=8), :] = (
            speed + COUPLE_STEP * (PARTICLE_DRAG * gas - slope)
        ) / (1.0 + COUPLE_STEP * PARTICLE_DRAG)


def gas_and_sample(gas, deposits, state):
    wide = B + 2 * WD
    ring = 2 * S
    return pl.pallas_call(
        gas_kernel,
        out_shape=[
            pltpu.VMEM((PZ * 8, S), jnp.float32),
            jax.ShapeDtypeStruct((3 * 64, S), jnp.float32),
            jax.ShapeDtypeStruct((64, S), jnp.float32),
        ],
        scratch_shapes=[
            pltpu.VMEM((4, B + 2 * WG, 24, ring), jnp.float32),
            pltpu.VMEM((B + 2 * WG, 24, S), jnp.float32),
            pltpu.VMEM((4, wide, wide, ring), jnp.float32),
            pltpu.VMEM((wide, wide, S), jnp.float32),
            pltpu.VMEM((3, wide, wide, ring), jnp.float32),
            pltpu.VMEM((3, wide, wide, ring), jnp.float32),
            pltpu.VMEM((wide, wide, ring), jnp.float32),
            pltpu.VMEM((wide, wide, ring), jnp.float32),
            pltpu.VMEM((wide, wide, ring), jnp.float32),
            pltpu.VMEM((wide, wide, ring), jnp.float32),
            pltpu.VMEM((3 * 64, S), jnp.float32),
            pltpu.VMEM((S, 3 * S), jnp.float32),
            pltpu.VMEM((4, S, 2 * S), jnp.float32),
            pltpu.VMEM((96, S), jnp.float32),
        ],
        name="gas_sample",
    )(*near((*gas, *deposits, state)))


def body(position, velocity, radius, cell_count, gas_velocity, pressure):
    rank = lax.axis_index("gz")
    count = lax.axis_size("gz")
    gas = jnp.concatenate([gas_velocity, pressure[None]], axis=0)
    sent = pack(
        cell_count.reshape(PZ),
        position.reshape(3 * PZ, S),
        velocity.reshape(3 * PZ, S),
        radius.reshape(PZ, S),
        gas_velocity.reshape(3 * B * B, S),
        pressure.reshape(B * B, S),
    )
    got = lax.all_to_all(sent, "gz", split_axis=0, concat_axis=0, tiled=True)
    got = got.reshape(PZ, 24, S)
    layers = jnp.concatenate([got[PZ - 3 :, 7:14], got[:, :7], got[:3, 7:14]], axis=0)
    own = jnp.swapaxes(layers, 0, 1).reshape(7 * L0, S)
    from_low = lax.dynamic_index_in_dim(got, jnp.maximum(rank - 1, 0), 0, keepdims=False)
    from_high = lax.dynamic_index_in_dim(got, jnp.minimum(rank + 1, count - 1), 0, keepdims=False)
    def edge(rows, there):
        rows = jnp.where(there, rows[14:], 0.0).reshape(2, WG, 2, B * B)
        return jnp.transpose(rows, (0, 2, 3, 1)).reshape(4, B * B, WG)

    zlo = edge(from_low, rank > 0)
    zhi = edge(from_high, rank < count - 1)
    packed = jnp.concatenate([zhi, jnp.zeros((4, B * B, 32 - 2 * WG), jnp.float32), zlo], axis=2)
    packed = jnp.swapaxes(packed, 0, 1).reshape(B * B, S)
    gas5 = jnp.concatenate([gas.reshape(4 * B * B, S), packed], axis=0)

    def y_slab(first):
        return gas5.reshape(5, B, B, S)[:, :, first : first + WG].reshape(5 * B * WG, S)

    def x_slab(ylo, yhi, first, at, width, block):
        parts = [block.reshape(5, B, B * S)[:, first : first + width].reshape(-1, S)]
        for part in (ylo, yhi):
            part = part[at:].reshape(5, B, width * S)[:, first : first + width]
            parts.append(part.reshape(-1, S))
        return parts

    ylo, yhi = shift_pair(own, own, "gy")
    column = jnp.concatenate([ylo, own, yhi], axis=0)
    xlo, xhi = shift_pair(column, column, "gx")
    first = (own, ylo, yhi, xlo, xhi)
    (moved,) = contact(L1, False, first, first)

    gylo, gyhi = shift_pair(y_slab(0), y_slab(B - WG), "gy")
    ylo, yhi = shift_pair(moved, moved, "gy")
    gxlo, gxhi = shift_pair(
        jnp.concatenate(x_slab(gylo, gyhi, 0, 0, WG, gas5), axis=0),
        jnp.concatenate(x_slab(gylo, gyhi, B - WG, 0, WG, gas5), axis=0),
        "gx",
    )
    column = jnp.concatenate([ylo, moved, yhi], axis=0)
    xlo, xhi = shift_pair(column, column, "gx")
    final, dep, dep_low, dep_high = contact(L2, True, (moved, ylo, yhi, xlo, xhi), first)

    dylo, dyhi = shift_pair(dep_low, dep_high, "gy")
    dxlo, dxhi = shift_pair(
        jnp.concatenate(x_slab(dylo, dyhi, 0, 0, WD, dep), axis=0),
        jnp.concatenate(x_slab(dylo, dyhi, B - WD, 0, WD, dep), axis=0),
        "gx",
    )
    sent_back, new_velocity, new_pressure = gas_and_sample(
        (gas5, gylo, gyhi, gxlo, gxhi), (dep, dylo, dyhi, dxlo, dxhi), final
    )
    returned = lax.all_to_all(sent_back, "gz", split_axis=0, concat_axis=0, tiled=True)
    place, speed = unpack(returned)
    return (
        place.reshape(3, 1, 1, PZ, S),
        speed.reshape(3, 1, 1, PZ, S),
        new_velocity.reshape(3, B, B, S),
        new_pressure.reshape(B, B, S),
    )


def solution(mesh):
    placed = (
        P(None, "gx", "gy", "gz", None),
        P(None, "gx", "gy", "gz", None),
        P("gx", "gy", "gz", None),
        P("gx", "gy", "gz"),
        P(None, "gx", "gy", "gz"),
        P("gx", "gy", "gz"),
    )
    return jax.shard_map(
        body,
        mesh=mesh,
        in_specs=placed,
        out_specs=(
            P(None, "gx", "gy", "gz", None),
            P(None, "gx", "gy", "gz", None),
            P(None, "gx", "gy", "gz"),
            P("gx", "gy", "gz"),
        ),
        check_vma=False,
    )
```

```python
import math

import jax
import jax.numpy as jnp
from jax import lax
from jax.experimental import pallas as pl
from jax.experimental.pallas import tpu as pltpu
from jax.sharding import PartitionSpec as P

B = 8
S = 128
PZ = 16
SWEEPS = 3
DAMPING = 0.5
TIME_STEP = 0.005
GRAVITY = 1.0
SOFTENING = 0.0025
GAS_STEP = 0.2
GAS_DRAG = 2.0
PARTICLE_DRAG = 4.0
COUPLE_STEP = 0.25
LOWER_BOUND = 0.2
UPPER_BOUND = 2.0

REACH = 0.194
FAR = 1e30
NEAR = tuple((dx, dy, dz) for dx in (-1, 0, 1) for dy in (-1, 0, 1) for dz in (-1, 0, 1))
HIGHEST = lax.Precision.HIGHEST
FLAGS = {}

L0 = PZ + 6
L1 = PZ + 4
L2 = PZ + 2
RADIUS_ROW = 6 * L0
WG = 5
WD = 4


def shift_pair(array_low, array_high, axis):
    count = lax.axis_size(axis)
    forward = [(i, (i + 1) % count) for i in range(count)]
    backward = [((i + 1) % count, i) for i in range(count)]
    from_below = lax.ppermute(array_high, axis, forward)
    from_above = lax.ppermute(array_low, axis, backward)
    return from_below, from_above


def chebyshev_factor(sweep_index, sweeps):
    centre = 0.5 * (UPPER_BOUND + LOWER_BOUND)
    radius_half = 0.5 * (UPPER_BOUND - LOWER_BOUND)
    return 1.0 / (centre + radius_half * math.cos(math.pi * (2 * sweep_index + 1) / (2 * sweeps)))


def has_sides():
    ranks = [lax.axis_index(axis) for axis in ("gx", "gy")]
    sizes = [lax.axis_size(axis) for axis in ("gx", "gy")]
    return tuple((r > 0, r >= 0, r < n - 1) for r, n in zip(ranks, sizes))


def lane_iota(rows):
    return lax.broadcasted_iota(jnp.int32, (rows, S), 1)


def axis_weights(row):
    centres = lax.broadcasted_iota(jnp.int32, (B, S), 0).astype(jnp.float32) + 0.5
    gap = jnp.broadcast_to(row, (B, S)) * float(B) - centres
    kernel = jnp.exp(-gap * gap)
    return kernel / jnp.sum(kernel, axis=0, keepdims=True)


def plane_weights(row_x, row_y):
    wx = axis_weights(row_x)
    wy = axis_weights(row_y)
    return jnp.concatenate(
        [jnp.broadcast_to(wx[a : a + 1], (B, S)) * wy for a in range(B)], axis=0
    )


def contact_kernel(cells, deposit, *refs):
    p_own, p_ylo, p_yhi, p_xlo, p_xhi, r_own, r_ylo, r_yhi, r_xlo, r_xhi = refs[:10]
    out_ref = refs[10]
    rest = refs[11:]
    if deposit:
        dep_ref, dep_lo_ref, dep_hi_ref = rest[:3]
        rest = rest[3:]
    mask_s, pref_s, work_s, key_s, list_s, own_s, turn_s, pick_s = rest[:8]
    cell_a, cell_b, acc_a, acc_b, force_s, rows_s, slots_s = rest[8:15]
    sides = has_sides()
    least = {
        (dx, dy): jnp.where(sides[0][dx + 1] & sides[1][dy + 1], 0.0, FAR)
        for dx in (-1, 0, 1)
        for dy in (-1, 0, 1)
    }
    layers = cells + 2
    shift = (L0 - cells) // 2
    block = 7 * L0 if cells == L1 else 6 * L1

    def source(dx, dy):
        if dx == 0:
            return ((p_ylo, p_own, p_yhi)[dy + 1], 0, (r_ylo, r_own, r_yhi)[dy + 1], RADIUS_ROW)
        p_ref, r_ref = (p_xlo, r_xlo) if dx < 0 else (p_xhi, r_xhi)
        return p_ref, (dy + 1) * block, r_ref, (dy + 1) * 7 * L0 + RADIUS_ROW

    lane = lane_iota(8)
    tri_row = lax.broadcasted_iota(jnp.int32, (S, 2 * S), 0)
    tri_col = lax.broadcasted_iota(jnp.int32, (S, 2 * S), 1)
    tri = jnp.where((tri_row < tri_col) | (tri_col >= S), 1.0, 0.0).astype(jnp.bfloat16)

    for start in (0, 8, cells - 8):
        own_r = r_own[RADIUS_ROW + shift + start : RADIUS_ROW + shift + start + 8, :]
        own_live = own_r > 0.0
        bounds = []
        for f in range(3):
            first = f * layers + 1 + start
            value = p_own[first : first + 8, :]
            top = jnp.max(jnp.where(own_live, value, -FAR), axis=1, keepdims=True) + REACH
            bottom = jnp.min(jnp.where(own_live, value, FAR), axis=1, keepdims=True) - REACH
            bounds.append((jnp.broadcast_to(bottom, (8, S)), jnp.broadcast_to(top, (8, S))))
        used = jnp.max(
            jnp.where(own_live, (lane + 1).astype(jnp.float32), 0.0), axis=1, keepdims=True
        )
        for k, offset in enumerate(NEAR):
            p_ref, p_base, r_ref, r_base = source(offset[0], offset[1])
            row = r_base + shift + start + offset[2]
            keep = r_ref[row : row + 8, :] > least[offset[:2]]
            for f in range(3):
                row = p_base + f * layers + 1 + start + offset[2]
                value = p_ref[row : row + 8, :] + float(offset[f])
                keep = keep & (value >= bounds[f][0]) & (value <= bounds[f][1])
            mask_s[k * 8 : k * 8 + 8, :] = jnp.where(keep, 1.0, 0.0)
        pref_s[...] = jnp.dot(
            mask_s[...].astype(jnp.bfloat16), tri, preferred_element_type=jnp.float32
        )
        base = jnp.zeros((8, S), jnp.int32)
        for k, offset in enumerate(NEAR):
            before = pref_s[k * 8 : k * 8 + 8, 0:S].astype(jnp.int32)
            count = pref_s[k * 8 : k * 8 + 8, S : 2 * S].astype(jnp.int32)
            hop = jnp.where(mask_s[k * 8 : k * 8 + 8, :] > 0.0, lane - before, 0)
            for bit in range(7):
                step = 1 << bit
                moved = pltpu.roll(hop, S - step, 1)
                hop = jnp.where(
                    (moved & step) != 0, moved, jnp.where((hop & step) != 0, 0, hop)
                )
            slot = (lane - base) & (S - 1)
            pick = (jnp.take_along_axis(hop, slot, axis=1) + slot) & (S - 1)
            page = (base >> 7) + jnp.where(lane < (base & (S - 1)), 1, 0)
            key_s[k * 8 : k * 8 + 8, :] = jnp.where(slot < count, page, -1)
            base = base + count
            p_ref, p_base, r_ref, r_base = source(offset[0], offset[1])
            for f in range(7):
                if f < 6:
                    row = p_base + f * layers + 1 + start + offset[2]
                    value = p_ref[row : row + 8, :]
                    if f < 3 and offset[f] != 0:
                        value = value + float(offset[f])
                else:
                    row = r_base + shift + start + offset[2]
                    value = r_ref[row : row + 8, :]
                work_s[k, f] = jnp.take_along_axis(value, pick, axis=1)
        total = base.astype(jnp.float32)
        pages = (jnp.max(total).astype(jnp.int32) + (S - 1)) >> 7
        for i in range(8):
            rows_s[start + i] = (
                jnp.max(total[i : i + 1, :]).astype(jnp.int32) + (S - 1)
            ) >> 7
            slots_s[start + i] = jnp.max(used[i : i + 1, :]).astype(jnp.int32)

        def merge(page, carry):
            acc = [jnp.zeros((8, S), jnp.float32)] * 6 + [jnp.full((8, S), -10.0, jnp.float32)]
            for k in range(27):
                here = key_s[k * 8 : k * 8 + 8, :] == page
                acc = [jnp.where(here, work_s[k, f], acc[f]) for f in range(7)]
            for f in range(7):
                list_s[page, f, start : start + 8, :] = acc[f]
            return carry

        lax.fori_loop(0, pages, merge, 0)

    radius = r_own[RADIUS_ROW + shift : RADIUS_ROW + shift + cells, :]
    live = radius > 0.0
    own_s[...] = jnp.zeros(own_s.shape, jnp.float32)
    for f in range(7):
        value = (
            p_own[f * layers + 1 : f * layers + 1 + cells, :]
            if f < 6
            else jnp.where(live, radius, -10.0)
        )
        for part in range(3):
            piece = value.astype(jnp.bfloat16).astype(jnp.float32)
            own_s[pl.ds(part * 8 + f, cells, stride=32), :] = piece
            value = value - piece
    for i in range(cells):
        turn_s[i] = own_s[i * 32 : i * 32 + 32, :].T.astype(jnp.bfloat16)
    pick_row = lax.broadcasted_iota(jnp.int32, (32, 7 * S), 0)
    pick_col = lax.broadcasted_iota(jnp.int32, (32, 7 * S), 1)
    chosen = (pick_row < 24) & ((pick_row & 7) == (pick_col >> 7))
    pick_s[...] = jnp.where(chosen, 1.0, 0.0).astype(jnp.bfloat16)
    force_s[...] = jnp.zeros((S, S), jnp.float32)

    def spread_cell(cell, target):
        target[...] = jnp.dot(
            turn_s[cell], pick_s[...], preferred_element_type=jnp.float32
        )

    def near_pages(cell, pages, values, sums, tiles, fresh):
        lists = [
            [jnp.broadcast_to(list_s[page, f, pl.ds(cell, 1), :], (8, S)) for f in range(7)]
            for page in pages
        ]
        for t in range(tiles):
            rows = slice(8 * t, 8 * t + 8)
            own = [values[rows, f * S : f * S + S] for f in range(7)]
            total = None
            for near in lists:
                part = pair_force(near, own)
                total = part if total is None else [a + b for a, b in zip(total, part)]
            for f in range(3):
                cols = slice(f * S, f * S + S)
                sums[rows, cols] = total[f] if fresh else sums[rows, cols] + total[f]

    def pair_force(near, own):
        ex = near[0] - own[0]
        ey = near[1] - own[1]
        ez = near[2] - own[2]
        square = ex * ex + ey * ey + ez * ez + SOFTENING
        inverse = lax.rsqrt(square)
        press = jnp.maximum((near[6] + own[6]) - square * inverse, 0.0)
        closing = (
            (near[3] - own[3]) * ex + (near[4] - own[4]) * ey + (near[5] - own[5]) * ez
        )
        size = press * inverse * (1.0 - DAMPING * (closing * inverse))
        return size * ex, size * ey, size * ez

    def reduce_cell(cell, sums):
        for t in range(16):
            rows = slice(8 * t, 8 * t + 8)
            tile = force_s[rows, :]
            for f in range(3):
                total_f = jnp.sum(sums[rows, f * S : f * S + S], axis=1, keepdims=True)
                tile = jnp.where(
                    lane == f * 32 + cell, jnp.broadcast_to(total_f, (8, S)), tile
                )
            force_s[rows, :] = tile

    def one_cell(cell, values, next_values, sums, last_sums):
        spread_cell(jnp.minimum(cell + 1, cells - 1), next_values)
        reduce_cell(cell - 1, last_sums)
        near_pages(cell, (0,), values, sums, 16, True)
        few = slots_s[cell] <= 64
        page_count = rows_s[cell]

        def more(tiles):
            def step(pair, carry):
                pages = (2 * pair - 1, 2 * pair)
                near_pages(cell, pages, values, sums, tiles, False)
                return carry

            lax.fori_loop(1, (page_count + 1) >> 1, step, 0)

            @pl.when((page_count > 1) & ((page_count & 1) == 0))
            def _():
                near_pages(cell, (page_count - 1,), values, sums, tiles, False)

        @pl.when(few)
        def _():
            more(8)

        @pl.when(jnp.logical_not(few))
        def _():
            more(16)

    def two_cells(pair, carry):
        one_cell(2 * pair, cell_a, cell_b, acc_a, acc_b)
        one_cell(2 * pair + 1, cell_b, cell_a, acc_b, acc_a)
        return carry

    spread_cell(0, cell_a)
    lax.fori_loop(0, cells // 2, two_cells, 0)
    reduce_cell(cells - 1, acc_b)

    force = force_s[...].T
    scale = jnp.where(live, -1.0 / (radius * radius * radius), 0.0)
    for f in range(3):
        push = force[f * 32 : f * 32 + cells, :] * scale
        if f == 2:
            push = push - GRAVITY
        first = (3 + f) * layers + 1
        speed = p_own[first : first + cells, :] + TIME_STEP * push
        first = f * layers + 1
        place = p_own[first : first + cells, :] + TIME_STEP * speed
        out_ref[f * cells : f * cells + cells, :] = place
        out_ref[(3 + f) * cells : (3 + f) * cells + cells, :] = speed

    if deposit:
        dep_s, edge_s = rest[15:17]

        def one_deposit(cell):
            def row(f):
                return out_ref[pl.ds(f * cells + cell, 1), :]

            r = r_own[pl.ds(RADIUS_ROW + shift + cell, 1), :]
            volume = (4.0 * math.pi / 3.0 * B**3) * (r * r * r)
            plane = plane_weights(row(0), row(1))
            wz = axis_weights(row(2))
            carried = [volume, volume * row(3), volume * row(4), volume * row(5)]
            left = jnp.concatenate(
                [jnp.broadcast_to(c, (B, S)) * wz for c in carried], axis=0
            )
            return lax.dot_general(
                left,
                plane,
                (((1,), (1,)), ((), ())),
                precision=HIGHEST,
                preferred_element_type=jnp.float32,
            )

        def some_deposits(step, carry):
            blocks = [one_deposit(step * 3 + i) for i in range(3)]
            for i in range(3):
                for f in range(4):
                    dep_s[f, pl.ds(pl.multiple_of(step * 24 + i * 8, 8), 8), 0:64] = blocks[i][
                        f * 8 : f * 8 + 8, :
                    ]
            return carry

        lax.fori_loop(0, cells // 3, some_deposits, 0)
        edge_s[...] = jnp.zeros((S, S), jnp.float32)
        for f in range(4):
            edge_s[f * 32 : f * 32 + 8, :] = dep_s[f, B + S : B + S + 8, :]
            edge_s[f * 32 + 24 : f * 32 + 32, :] = dep_s[f, 0:B, :]
        for f in range(5):
            grid = (dep_s[f, B : B + S, :] if f < 4 else edge_s[...]).T
            dep_ref[f * 64 : f * 64 + 64, :] = grid[0:64, :]
            for x in range(B):
                row = (f * B + x) * WD
                dep_lo_ref[row : row + WD, :] = grid[x * B : x * B + WD, :]
                dep_hi_ref[row : row + WD, :] = grid[x * B + B - WD : x * B + B, :]


def pack_kernel(count_ref, pos_ref, vel_ref, rad_ref, gas_ref, prs_ref, out_ref):
    rank = lax.axis_index("gz")
    row = lax.broadcasted_iota(jnp.int32, (PZ, S), 0)
    counts = jnp.zeros((PZ, S), jnp.int32)
    for i in range(PZ):
        counts = jnp.where(row == i, count_ref[i], counts)
    live = lane_iota(PZ) < counts
    fields = [pos_ref[f * PZ : f * PZ + PZ, :] for f in range(3)]
    fields += [vel_ref[f * PZ : f * PZ + PZ, :] for f in range(3)]
    fields.append(jnp.where(live, rad_ref[...], 0.0))
    lower = rank >= PZ - 3
    for f in range(7):
        out_ref[pl.ds(f, PZ, stride=24), :] = fields[f]
        below = jnp.where(row == 0, 0.0, pltpu.roll(fields[f], 1, 0))
        above = jnp.where(row == PZ - 1, 0.0, pltpu.roll(fields[f], PZ - 1, 0))
        out_ref[pl.ds(7 + f, PZ, stride=24), :] = jnp.where(lower, below, above)
    first = gas_ref[0:S, :].T
    second = jnp.concatenate([gas_ref[S : S + 64, :], prs_ref[...]], axis=0).T
    for target in range(PZ):
        up = jnp.where(rank + 1 == target, 1.0, 0.0)
        down = jnp.where(rank - 1 == target, 1.0, 0.0)
        for i, turned in enumerate((first, second)):
            at = target * 24 + 14 + i * WG
            out_ref[at : at + WG, :] = turned[S - WG :, :] * up + turned[:WG, :] * down


def pack(*arrays):
    return pl.pallas_call(
        pack_kernel,
        out_shape=pltpu.VMEM((PZ * 24, S), jnp.float32),
        in_specs=[pl.BlockSpec(memory_space=pltpu.SMEM)]
        + [pl.BlockSpec(memory_space=pltpu.VMEM)] * 5,
        name="pack",
    )(*arrays)


def unpack_kernel(got_ref, place_ref, speed_ref):
    for f in range(3):
        place_ref[f * PZ : f * PZ + PZ, :] = got_ref[pl.ds(f, PZ, stride=8), :]
        speed_ref[f * PZ : f * PZ + PZ, :] = got_ref[pl.ds(3 + f, PZ, stride=8), :]


def unpack(got):
    return pl.pallas_call(
        unpack_kernel,
        out_shape=[jax.ShapeDtypeStruct((3 * PZ, S), jnp.float32)] * 2,
        name="unpack",
    )(*near([got]))


def near(arrays):
    return [pltpu.with_memory_space_constraint(a, pltpu.VMEM) for a in arrays]


def contact(cells, deposit, places, radii):
    shapes = [pltpu.VMEM((6 * cells, S), jnp.float32)]
    scratch = [
        pltpu.VMEM((27 * 8, S), jnp.float32),
        pltpu.VMEM((27 * 8, 2 * S), jnp.float32),
        pltpu.VMEM((27, 7, 8, S), jnp.float32),
        pltpu.VMEM((27 * 8, S), jnp.int32),
        pltpu.VMEM((27, 7, 24, S), jnp.float32),
        pltpu.VMEM((5 * S, S), jnp.float32),
        pltpu.VMEM((L1, S, 32), jnp.bfloat16),
        pltpu.VMEM((32, 7 * S), jnp.bfloat16),
        pltpu.VMEM((S, 7 * S), jnp.float32),
        pltpu.VMEM((S, 7 * S), jnp.float32),
        pltpu.VMEM((S, 3 * S), jnp.float32),
        pltpu.VMEM((S, 3 * S), jnp.float32),
        pltpu.VMEM((S, S), jnp.float32),
        pltpu.SMEM((24,), jnp.int32),
        pltpu.SMEM((24,), jnp.int32),
    ]
    if deposit:
        shapes.append(pltpu.VMEM((5 * 64, S), jnp.float32))
        shapes += [pltpu.VMEM((5 * B * WD, S), jnp.float32)] * 2
        scratch += [pltpu.VMEM((4, S + 2 * B, S), jnp.float32), pltpu.VMEM((S, S), jnp.float32)]
    return pl.pallas_call(
        lambda *refs: contact_kernel(cells, deposit, *refs),
        out_shape=shapes,
        scratch_shapes=scratch,
        compiler_params=pltpu.CompilerParams(flags=FLAGS),
        name="contact_deposit" if deposit else "contact",
    )(*near(places), *near(radii))


def assemble(target, edge, own, ylo, yhi, xlo, xhi, y_at, x_at, width, weight):
    span = B + 2 * width

    def put(field, x, y, value):
        rows = slice(y, y + value.shape[0])
        if field < 4:
            target[field, x, rows, 0:S] = value
        else:
            edge[x, rows, :] = value

    for field in range(5):
        for x in range(B):
            row = (field * B + x) * B
            put(field, width + x, width, own[row : row + B, :])
            row = y_at + (field * B + x) * width
            put(field, width + x, 0, ylo[row : row + width, :] * weight[0, -1])
            put(field, width + x, width + B, yhi[row : row + width, :] * weight[0, 1])
        for x in range(width):
            for place, ref, side in ((x, xlo, -1), (width + B + x, xhi, 1)):
                row = x_at + (field * width + x) * B
                put(field, place, width, ref[row : row + B, :] * weight[side, 0])
        reach = width - 1
        for x in range(reach):
            for place, ref, side in ((width - reach + x, xlo, -1), (width + B + x, xhi, 1)):
                row = x_at + 5 * width * B + (field * reach + x) * reach
                put(field, place, width - reach, ref[row : row + reach, :] * weight[side, -1])
                row += 5 * reach * reach
                put(field, place, width + B, ref[row : row + reach, :] * weight[side, 1])
    lane = lane_iota(8)
    for field in range(4):
        index = field * 32 + jnp.where(
            lane < 64, jnp.minimum(lane, 15), jnp.maximum(lane - 96, 16)
        )
        for x in range(span):
            for y in range(0, edge.shape[1], 8):
                target[field, x, y : y + 8, S : 2 * S] = jnp.take_along_axis(
                    edge[x, y : y + 8, :], index, axis=1
                )


def gas_kernel(*refs):
    (
        g_own,
        g_ylo,
        g_yhi,
        g_xlo,
        g_xhi,
        d_own,
        d_ylo,
        d_yhi,
        d_xlo,
        d_xhi,
        state_ref,
        sent_ref,
        newv_ref,
        newp_ref,
        u_s,
        ue_s,
        d_s,
        de_s,
        flux_s,
        mid_s,
        inv_s,
        src_s,
        pa_s,
        pb_s,
        grad_s,
        field_s,
        pair_s,
        sum_s,
    ) = refs
    sides = has_sides()
    weight = {
        (dx, dy): jnp.where(sides[0][dx + 1] & sides[1][dy + 1], 1.0, 0.0)
        for dx in (-1, 0, 1)
        for dy in (-1, 0, 1)
    }
    assemble(u_s, ue_s, g_own, g_ylo, g_yhi, g_xlo, g_xhi, 0, 0, WG, weight)
    assemble(d_s, de_s, d_own, d_ylo, d_yhi, d_xlo, d_xhi, 0, 0, WD, weight)
    wide = B + 2 * WD
    ring = 2 * S

    def zdiff(value):
        return pltpu.roll(value, ring - 1, 1) - pltpu.roll(value, 1, 1)

    def zsum(value):
        return pltpu.roll(value, ring - 1, 1) + pltpu.roll(value, 1, 1)

    def ydiff(value):
        return pltpu.roll(value, wide - 1, 0) - pltpu.roll(value, 1, 0)

    def ysum(value):
        return pltpu.roll(value, wide - 1, 0) + pltpu.roll(value, 1, 0)

    for x in range(wide):
        speed = [u_s[d, x + 1, 1 : wide + 1, :] for d in range(3)]
        solids = d_s[0, x]
        voidage = 1.0 / (1.0 + solids)
        under = 1.0 / (voidage + GAS_STEP * GAS_DRAG * solids)
        inv_s[x] = 1.0 / (6.0 + voidage)
        for k in range(3):
            slope = speed[0] * (u_s[k, x + 2, 1 : wide + 1, :] - u_s[k, x, 1 : wide + 1, :])
            slope += speed[1] * (u_s[k, x + 1, 2 : wide + 2, :] - u_s[k, x + 1, 0:wide, :])
            slope += speed[2] * zdiff(speed[k])
            pulled = speed[k] - (0.5 * GAS_STEP) * slope
            middle = (voidage * pulled + GAS_STEP * GAS_DRAG * d_s[1 + k, x]) * under
            mid_s[k, x] = middle
            flux_s[k, x] = voidage * middle
        pa_s[x] = u_s[3, x + 1, 1 : wide + 1, :]
    for x in range(1, wide - 1):
        spread = (flux_s[0, x + 1] - flux_s[0, x - 1]) + ydiff(flux_s[1, x]) + zdiff(flux_s[2, x])
        src_s[x] = (-0.5 / GAS_STEP) * spread * inv_s[x]

    row = lax.broadcasted_iota(jnp.int32, (wide, ring), 0) - WD + lax.axis_index("gy") * B
    col = lax.broadcasted_iota(jnp.int32, (wide, ring), 1)
    col = jnp.where(col < ring - 64, col, col - ring) + lax.axis_index("gz") * S
    limits = (lax.axis_size("gx") * B, lax.axis_size("gy") * B, lax.axis_size("gz") * S)
    inside = (row >= 0) & (row < limits[1]) & (col >= 0) & (col < limits[2])
    for sweep in range(SWEEPS):
        old, new = (pa_s, pb_s) if sweep % 2 == 0 else (pb_s, pa_s)
        factor = chebyshev_factor(sweep, SWEEPS)
        for x in range(1 + sweep, wide - 1 - sweep):
            place = lax.axis_index("gx") * B + (x - WD)
            kept = jnp.where((place >= 0) & (place < limits[0]), 1.0, 0.0)
            middle = old[x]
            around = (old[x + 1] + old[x - 1]) + ysum(middle) + zsum(middle)
            value = middle + factor * (src_s[x] + around * inv_s[x] - middle)
            new[x] = jnp.where(inside, value, 0.0) * kept
    last = pb_s if SWEEPS % 2 == 1 else pa_s
    rows = slice(WD, WD + B)
    for x in range(B):
        plane = last[WD + x]
        slopes = (last[WD + x + 1] - last[WD + x - 1], ydiff(plane), zdiff(plane))
        newp_ref[x * B : x * B + B, :] = plane[rows, 0:S]
        for k in range(3):
            slope = 0.5 * slopes[k]
            at = (k * B + x) * B
            grad_s[at : at + B, :] = slope[rows, 0:S]
            newv_ref[at : at + B, :] = (mid_s[k, WD + x] - GAS_STEP * slope)[rows, 0:S]

    joined = (
        newv_ref[0:S, :],
        jnp.concatenate([newv_ref[S : S + 64, :], grad_s[0:64, :]], axis=0),
        grad_s[64:192, :],
    )
    for v in range(3):
        field_s[:, v * S : v * S + S] = joined[v].T
    pair_s[...] = jnp.zeros((4, S, 2 * S), jnp.float32)

    def some_cells(step, carry):
        for i in range(4):
            cell = step * 4 + i

            def row_of(f):
                return state_ref[pl.ds(f * L2 + 1 + cell, 1), :]

            plane_w = plane_weights(row_of(0), row_of(1))
            wz = axis_weights(row_of(2))
            pair_s[i, 0:64, 0:S] = plane_w
            pair_s[i, 64:S, S : 2 * S] = plane_w
            start = pl.multiple_of(cell * 8, 8)
            left = jnp.concatenate(
                [field_s[pl.ds(start, 8), v * S : v * S + S] for v in range(3)], axis=0
            )
            part = jnp.dot(
                left, pair_s[i], precision=HIGHEST, preferred_element_type=jnp.float32
            )
            for v in range(3):
                for odd in range(2):
                    value = part[v * 8 : v * 8 + 8, odd * S : odd * S + S] * wz
                    sum_s[pl.ds((2 * v + odd) * 16 + cell, 1), :] = jnp.sum(
                        value, axis=0, keepdims=True
                    )
        return carry

    lax.fori_loop(0, PZ // 4, some_cells, 0)
    for f in range(3):
        speed = state_ref[(3 + f) * L2 + 1 : (3 + f) * L2 + 17, :]
        gas = sum_s[f * 16 : f * 16 + 16, :]
        slope = sum_s[(3 + f) * 16 : (3 + f) * 16 + 16, :]
        sent_ref[pl.ds(f, PZ, stride=8), :] = state_ref[f * L2 + 1 : f * L2 + 17, :]
        sent_ref[pl.ds(3 + f, PZ, stride=8), :] = (
            speed + COUPLE_STEP * (PARTICLE_DRAG * gas - slope)
        ) / (1.0 + COUPLE_STEP * PARTICLE_DRAG)


def gas_and_sample(gas, deposits, state):
    wide = B + 2 * WD
    ring = 2 * S
    return pl.pallas_call(
        gas_kernel,
        out_shape=[
            pltpu.VMEM((PZ * 8, S), jnp.float32),
            jax.ShapeDtypeStruct((3 * 64, S), jnp.float32),
            jax.ShapeDtypeStruct((64, S), jnp.float32),
        ],
        scratch_shapes=[
            pltpu.VMEM((4, B + 2 * WG, 24, ring), jnp.float32),
            pltpu.VMEM((B + 2 * WG, 24, S), jnp.float32),
            pltpu.VMEM((4, wide, wide, ring), jnp.float32),
            pltpu.VMEM((wide, wide, S), jnp.float32),
            pltpu.VMEM((3, wide, wide, ring), jnp.float32),
            pltpu.VMEM((3, wide, wide, ring), jnp.float32),
            pltpu.VMEM((wide, wide, ring), jnp.float32),
            pltpu.VMEM((wide, wide, ring), jnp.float32),
            pltpu.VMEM((wide, wide, ring), jnp.float32),
            pltpu.VMEM((wide, wide, ring), jnp.float32),
            pltpu.VMEM((3 * 64, S), jnp.float32),
            pltpu.VMEM((S, 3 * S), jnp.float32),
            pltpu.VMEM((4, S, 2 * S), jnp.float32),
            pltpu.VMEM((96, S), jnp.float32),
        ],
        name="gas_sample",
    )(*near((*gas, *deposits, state)))


def body(position, velocity, radius, cell_count, gas_velocity, pressure):
    rank = lax.axis_index("gz")
    count = lax.axis_size("gz")
    gas = jnp.concatenate([gas_velocity, pressure[None]], axis=0)
    sent = pack(
        cell_count.reshape(PZ),
        position.reshape(3 * PZ, S),
        velocity.reshape(3 * PZ, S),
        radius.reshape(PZ, S),
        gas_velocity.reshape(3 * B * B, S),
        pressure.reshape(B * B, S),
    )
    got = lax.all_to_all(sent, "gz", split_axis=0, concat_axis=0, tiled=True)
    got = got.reshape(PZ, 24, S)
    layers = jnp.concatenate([got[PZ - 3 :, 7:14], got[:, :7], got[:3, 7:14]], axis=0)
    own = jnp.swapaxes(layers, 0, 1).reshape(7 * L0, S)
    from_low = lax.dynamic_index_in_dim(got, jnp.maximum(rank - 1, 0), 0, keepdims=False)
    from_high = lax.dynamic_index_in_dim(got, jnp.minimum(rank + 1, count - 1), 0, keepdims=False)
    def edge(rows, there):
        rows = jnp.where(there, rows[14:], 0.0).reshape(2, WG, 2, B * B)
        return jnp.transpose(rows, (0, 2, 3, 1)).reshape(4, B * B, WG)

    zlo = edge(from_low, rank > 0)
    zhi = edge(from_high, rank < count - 1)
    packed = jnp.concatenate([zhi, jnp.zeros((4, B * B, 32 - 2 * WG), jnp.float32), zlo], axis=2)
    packed = jnp.swapaxes(packed, 0, 1).reshape(B * B, S)
    gas5 = jnp.concatenate([gas.reshape(4 * B * B, S), packed], axis=0)

    def y_slab(first):
        return gas5.reshape(5, B, B, S)[:, :, first : first + WG].reshape(5 * B * WG, S)

    def x_slab(ylo, yhi, first, at, width, block):
        parts = [block.reshape(5, B, B * S)[:, first : first + width].reshape(-1, S)]
        reach = width - 1
        near_x = first if first == 0 else B - reach
        for part, near_y in ((ylo, width - reach), (yhi, 0)):
            part = part[at:].reshape(5, B, width, S)[:, near_x : near_x + reach]
            parts.append(part[:, :, near_y : near_y + reach].reshape(-1, S))
        return parts

    ylo, yhi = shift_pair(own, own, "gy")
    column = jnp.concatenate([ylo, own, yhi], axis=0)
    xlo, xhi = shift_pair(column, column, "gx")
    first = (own, ylo, yhi, xlo, xhi)
    (moved,) = contact(L1, False, first, first)

    gylo, gyhi = shift_pair(y_slab(0), y_slab(B - WG), "gy")
    ylo, yhi = shift_pair(moved, moved, "gy")
    gxlo, gxhi = shift_pair(
        jnp.concatenate(x_slab(gylo, gyhi, 0, 0, WG, gas5), axis=0),
        jnp.concatenate(x_slab(gylo, gyhi, B - WG, 0, WG, gas5), axis=0),
        "gx",
    )
    column = jnp.concatenate([ylo, moved, yhi], axis=0)
    xlo, xhi = shift_pair(column, column, "gx")
    final, dep, dep_low, dep_high = contact(L2, True, (moved, ylo, yhi, xlo, xhi), first)

    dylo, dyhi = shift_pair(dep_low, dep_high, "gy")
    dxlo, dxhi = shift_pair(
        jnp.concatenate(x_slab(dylo, dyhi, 0, 0, WD, dep), axis=0),
        jnp.concatenate(x_slab(dylo, dyhi, B - WD, 0, WD, dep), axis=0),
        "gx",
    )
    sent_back, new_velocity, new_pressure = gas_and_sample(
        (gas5, gylo, gyhi, gxlo, gxhi), (dep, dylo, dyhi, dxlo, dxhi), final
    )
    returned = lax.all_to_all(sent_back, "gz", split_axis=0, concat_axis=0, tiled=True)
    place, speed = unpack(returned)
    return (
        place.reshape(3, 1, 1, PZ, S),
        speed.reshape(3, 1, 1, PZ, S),
        new_velocity.reshape(3, B, B, S),
        new_pressure.reshape(B, B, S),
    )


def solution(mesh):
    placed = (
        P(None, "gx", "gy", "gz", None),
        P(None, "gx", "gy", "gz", None),
        P("gx", "gy", "gz", None),
        P("gx", "gy", "gz"),
        P(None, "gx", "gy", "gz"),
        P("gx", "gy", "gz"),
    )
    return jax.shard_map(
        body,
        mesh=mesh,
        in_specs=placed,
        out_specs=(
            P(None, "gx", "gy", "gz", None),
            P(None, "gx", "gy", "gz", None),
            P(None, "gx", "gy", "gz"),
            P("gx", "gy", "gz"),
        ),
        check_vma=False,
    )
```
